32 devices in a mesh: mem: 4 (over x, core), band: 8 (over z, y).
Axes of the slice: x: 2, y: 2, z: 4, core: 2. Of those that a mesh axis runs over, the one named last changes fastest.
Arguments:
- sample_collection: float32 [24, 3, 64, 4096], P('mem', None, 'band'), may hold values from -6 to 6
- seabed_profile: float32 [64, 4096], P('band'), may hold values from 0.5 to 2
- gauge_grid_position: int32 [32, 128], P('band'), may hold values from 0 to 262143, as said below
- observed_values: float32 [32, 128], P('band'), may hold values from -6 to 6
- error_scale: float32 [32, 128], P('band'), may hold values from 0.3 to 3
- perturbation: float32 [24, 32, 128], P('mem', 'band'), may hold values from -6 to 6
- inflation: float32 [1], replicated, may hold values from 1 to 16
Outputs:
- analysis: float32 [24, 3, 64, 4096], P('mem', None, 'band')
The draws below stay inside these ranges and needn't reach their ends.
Inputs may be any that keep to these rules, and one draw needn't show every extreme that they name: Every entry in row r of gauge_grid_position lies in grid rows b * 8 to (b + 1) * 8 - 1 with b = r // 4; cells may repeat.
All inputs are finite; a program needn't handle non-finite values.
Results may differ from the reference program's by a relative error of at most 0.000071.
Values sent between devices are 32-bit elements; how exact they have to be, the bound alone decides.
No kernel may reach another device: no remote copies, remote signals or barrier semaphores. Data moves between devices by JAX's collectives and lax.ppermute only.
A program may use at most 128 MiB of HBM per device.

```python
import math
import jax
import jax.numpy as jnp
from jax import lax

ROWS = 8
NC = 4096
OBS_ROWS_DEV = 4
STEPS = 2
MEMBERS = 24
NY = 64
OBS_ROWS = 32


def draw_gauge_grid_position(key, part):
    band_of_row = jnp.arange(OBS_ROWS, dtype=jnp.int32) // OBS_ROWS_DEV
    offsets = jax.random.randint(key, (OBS_ROWS, 128), 0, ROWS * NC, dtype=jnp.int32)
    return band_of_row[:, None] * (ROWS * NC) + offsets


def shard_levels(key, extent, pieces, low, largest):
    loudness = 1.0
    for dim, parts in pieces:
        steps = jax.random.uniform(jax.random.fold_in(jax.random.fold_in(key, 6), dim), (parts,), jnp.float32, low / len(pieces), largest / len(pieces))
        loudness = loudness * jnp.repeat(jnp.exp(steps), extent[dim] // parts).reshape((-1,) + (1,) * (len(extent) - 1 - dim))
    return loudness


def noise(rng, shape, width, most, pieces=(), kind=jnp.bfloat16):
    entries = jax.random.normal(rng, shape, jnp.float32) * width
    if len(pieces) > 0:
        entries = shard_levels(rng, shape, pieces, -0.22, 0.18) * entries
    return jnp.clip(entries, min=-most, max=most).astype(kind)


def setup_inputs(seed: int = 0) -> dict:
    seeds = jax.random.split(jax.random.key(seed), 8)
    return {
        "sample_collection": noise(seeds[0], (MEMBERS, 3, NY, NC), 1.0, 6.0, ((0, 4), (2, 8)), jnp.float32),
        "seabed_profile": jnp.clip(jnp.exp(math.log(2.0) - 1.3862944 * jax.random.uniform(seeds[1], (NY, NC), jnp.float32) ** shard_levels(seeds[1], (NY, NC), ((0, 8),), -0.2, 0.2)), 0.5, 2.0),
        "gauge_grid_position": draw_gauge_grid_position(jax.random.fold_in(seeds[7], 71), 0),
        "observed_values": noise(seeds[3], (OBS_ROWS, 128), 1.0, 6.0, ((0, 8),), jnp.float32),
        "error_scale": jnp.clip(jnp.exp(math.log(3.0) - 2.3025851 * jax.random.uniform(seeds[4], (OBS_ROWS, 128), jnp.float32) ** shard_levels(seeds[4], (OBS_ROWS, 128), ((0, 8),), -0.2, 0.2)), 0.3, 3.0),
        "perturbation": noise(seeds[5], (MEMBERS, OBS_ROWS, 128), 1.0, 6.0, ((0, 4), (1, 8)), jnp.float32),
        "inflation": jnp.clip(jnp.exp(jax.random.uniform(seeds[6], (1,), jnp.float32, math.log(1.0), math.log(16.0))), 1.0, 16.0),
    }


courant = 0.5
coriolis_base = 0.15
coriolis_slope = 0.3

def east_diff(quantity):
    return (jnp.roll(quantity, -1, axis=-1) - jnp.roll(quantity, 1, axis=-1)) * 0.5

def north_diff(quantity):
    padded = jnp.pad(quantity, ((1, 1), (0, 0)))
    return (padded[2:] - padded[:-2]) * 0.5

def advance_one_sample(sample_trajectory, seabed_profile, earth_spin_turning):
    surface_height, eastward_velocity_field, northward_velocity_field = (sample_trajectory[0], sample_trajectory[1], sample_trajectory[2])
    for _ in range(STEPS):
        surface_height = surface_height - courant * (east_diff(seabed_profile * eastward_velocity_field) + north_diff(seabed_profile * northward_velocity_field))
        eastward_velocity_field = eastward_velocity_field - courant * east_diff(surface_height) + earth_spin_turning * northward_velocity_field
        northward_velocity_field = northward_velocity_field - courant * north_diff(surface_height) - earth_spin_turning * eastward_velocity_field
    return jnp.stack([surface_height, eastward_velocity_field, northward_velocity_field])

def reference(sample_collection, seabed_profile, gauge_grid_position, observed_values, error_scale, perturbation, inflation):
    sample_trajectories = sample_collection.shape[0]
    rows_index = jnp.arange(NY).astype(jnp.float32)
    earth_spin_turning = (coriolis_base + coriolis_slope * (rows_index + 0.5) / NY)[:, None]
    prior_model_outputs = lax.map(lambda sample_trajectory: advance_one_sample(sample_trajectory, seabed_profile, earth_spin_turning), sample_collection)
    modelled_water_levels = jnp.take(prior_model_outputs[:, 0].reshape(sample_trajectories, -1), gauge_grid_position.reshape(-1), axis=1)
    obs_scale = error_scale.reshape(-1)
    factor = inflation[0]
    innovation = (observed_values.reshape(-1) + jnp.sqrt(factor) * obs_scale * perturbation.reshape(sample_trajectories, -1) - modelled_water_levels) / obs_scale
    centre = lax.optimization_barrier(jnp.sum(modelled_water_levels, axis=0)) / sample_trajectories
    spread = (modelled_water_levels - centre) / (obs_scale * math.sqrt(sample_trajectories - 1))
    gram_matrix = jnp.dot(spread.astype(jnp.float32), spread.T.astype(jnp.float32), precision=lax.Precision.HIGHEST, preferred_element_type=jnp.float32)
    cross_term = jnp.dot(spread.astype(jnp.float32), innovation.T.astype(jnp.float32), precision=lax.Precision.HIGHEST, preferred_element_type=jnp.float32)
    system = gram_matrix + factor * jnp.eye(sample_trajectories, dtype=jnp.float32)
    cholesky_lower = jnp.linalg.cholesky(system)
    middle = lax.linalg.triangular_solve(cholesky_lower, cross_term, left_side=True, lower=True)
    weights = lax.linalg.triangular_solve(cholesky_lower, middle, left_side=True, lower=True, transpose_a=True)
    assimilate_update_step = jnp.eye(sample_trajectories, dtype=jnp.float32) + (weights - lax.optimization_barrier(jnp.mean(weights, axis=0, keepdims=True))) / math.sqrt(sample_trajectories - 1)
    return jnp.tensordot(assimilate_update_step, prior_model_outputs, axes=([0], [0]), precision=lax.Precision.HIGHEST)
```

```python
import functools
import math

import jax
import jax.numpy as jnp
from jax import lax
from jax.experimental import pallas as pl
from jax.experimental.pallas import tpu as pltpu
from jax.sharding import PartitionSpec as P

STEPS = 2
LANES = 128

courant = 0.5
coriolis_base = 0.15
coriolis_slope = 0.3


f32 = jnp.float32


def pad8(count):
    return -(-count // 8) * 8


def cost(flops, moved):
    return pl.CostEstimate(flops=flops, bytes_accessed=moved, transcendentals=0)


def shift_both(low_edge, high_edge):
    count = lax.axis_size("band")
    above = lax.ppermute(high_edge, "band", [(i, i + 1) for i in range(count - 1)])
    below = lax.ppermute(low_edge, "band", [(i + 1, i) for i in range(count - 1)])
    return above, below


def band_sum(part):
    count = lax.axis_size("band")
    if count & (count - 1):
        return lax.psum(part, "band")
    step = 1
    while step < count:
        part = part + lax.ppermute(part, "band", [(i, i ^ step) for i in range(count)])
        step *= 2
    return part


def mem_plan(count):
    if count % 2 or count == 1:
        return [(s, None) for s in range(1, count)]
    far = [(2 * s, None) for s in range(1, count // 2)]
    return far


def far_gather(block):
    count = lax.axis_size("mem")
    return [
        lax.ppermute(block, "mem", [(i, (i + s) % count) for i in range(count)])
        for s, _ in mem_plan(count)
    ]


def near_swap(block):
    count = lax.axis_size("mem")
    return lax.ppermute(block, "mem", [(i, i ^ 1) for i in range(count)])


def mem_gather(block):
    blocks = [block] + far_gather(block)
    if lax.axis_size("mem") % 2 == 0:
        blocks = blocks + [near_swap(b) for b in blocks]
    return blocks


def east(q):
    columns = q.shape[-1]
    return (pltpu.roll(q, columns - 1, 1) - pltpu.roll(q, 1, 1)) * 0.5


def north(q, above, below):
    rows = q.shape[0]
    index = lax.broadcasted_iota(jnp.int32, q.shape, 0)
    up = jnp.where(index == rows - 1, below, pltpu.roll(q, rows - 1, 0))
    down = jnp.where(index == 0, above, pltpu.roll(q, 1, 0))
    return (up - down) * 0.5


def spin(first_row, shape, total_rows):
    rows = (first_row + lax.broadcasted_iota(jnp.int32, shape, 0)).astype(f32)
    return coriolis_base + coriolis_slope * (rows + 0.5) / total_rows


def height_kernel(h_ref, u_ref, v_ref, b_ref, above_ref, below_ref, h_out, lo_out, hi_out):
    depth = b_ref[...]
    h = h_ref[...] - courant * (
        east(depth * u_ref[...]) + north(depth * v_ref[...], above_ref[...], below_ref[...])
    )
    h_out[...] = h
    lo_out[...] = h[:1]
    hi_out[...] = h[-1:]


def speed_kernel(
    total_rows, row_ref, h_ref, u_ref, v_ref, b_ref, above_ref, below_ref,
    u_out, v_out, w_out, lo_out, hi_out,
):
    h, v0 = h_ref[...], v_ref[...]
    turn = spin(row_ref[0], h.shape, total_rows)
    u = u_ref[...] - courant * east(h) + turn * v0
    v = v0 - courant * north(h, above_ref[...], below_ref[...]) - turn * u
    u_out[...] = u
    v_out[...] = v
    w_out[...] = u + turn * v
    flux = b_ref[...] * v
    lo_out[...] = flux[:1]
    hi_out[...] = flux[-1:]


def last_kernel(total_rows, row_ref, h_ref, w_ref, v_ref, above_ref, below_ref, v_out):
    h = h_ref[...]
    turn = spin(row_ref[0], h.shape, total_rows)
    u = w_ref[...] - courant * east(h)
    v_out[...] = v_ref[...] - courant * north(h, above_ref[...], below_ref[...]) - turn * u


def probe_kernel(cell_ref, h_ref, out_ref, cells):
    members, rows, columns = h_ref.shape
    chunks = columns // LANES
    if members % 8:
        cells[...] = jnp.zeros_like(cells)
    for m in range(members):
        for r in range(rows):
            for c in range(chunks):
                cells[r * chunks + c, m : m + 1, :] = h_ref[
                    m, r : r + 1, c * LANES : (c + 1) * LANES
                ]
    lane = lax.broadcasted_iota(jnp.int32, out_ref.shape[1:], 1)
    for k in range(out_ref.shape[0]):

        def take(i, held, k=k):
            cell = cell_ref[k, i]
            piece = cells[lax.shift_right_logical(cell, 7)]
            turned = pltpu.roll(piece, lax.rem(i - (cell & 127) + LANES, LANES), 1)
            return jnp.where(lane == i, turned, held)

        out_ref[k] = lax.fori_loop(
            0, LANES, take, jnp.zeros(out_ref.shape[1:], f32), unroll=8
        )


def gram_kernel(total, members, inf_ref, obs_ref, scale_ref, pert_ref, *refs):
    out_ref, spread, both = refs[-3:]
    groups = refs[:-3]
    padded = groups[0].shape[1]
    real = lax.broadcasted_iota(jnp.int32, (padded, LANES), 0) < members
    root = jnp.sqrt(jnp.full((1, LANES), inf_ref[0], f32))
    both[...] = jnp.zeros_like(both)
    for k in range(groups[0].shape[0]):
        at = slice(k * LANES, (k + 1) * LANES)
        scale = scale_ref[k : k + 1, :]
        sums = groups[0][k]
        for g in groups[1:]:
            sums = sums + g[k]
        centre = jnp.sum(sums, axis=0, keepdims=True) / total
        for n, g in enumerate(groups):
            s = jnp.where(real, (g[k] - centre) / (scale * math.sqrt(total - 1)), 0.0)
            spread[n * padded : (n + 1) * padded, at] = s
            both[n * padded : (n + 1) * padded, at] = s
        for m in range(members):
            both[len(groups) * padded + m : len(groups) * padded + m + 1, at] = (
                obs_ref[k : k + 1, :]
                + root * scale * pert_ref[m, k : k + 1, :]
                - groups[0][k, m : m + 1, :]
            ) / scale
    out_ref[...] = lax.dot_general(
        spread[...], both[...], (((1,), (1,)), ((), ())),
        precision=lax.Precision.HIGHEST, preferred_element_type=f32,
    )


def solve_kernel(total, members, groups, inf_ref, part_ref, out_ref):
    a = part_ref[...]
    size = a.shape[0]
    padded = size // groups
    row = lax.broadcasted_iota(jnp.int32, a.shape, 0)
    lane = lax.broadcasted_iota(jnp.int32, a.shape, 1)
    a = a + jnp.where(row == lane, inf_ref[0], 0.0)
    for g in range(groups):
        for m in range(members):
            k = g * padded + m
            pivot = a[k : k + 1, k : k + 1]
            inverse = 1.0 / jnp.sqrt(pivot)
            line = a[k : k + 1, :] * inverse
            column = a[:, k : k + 1] * inverse
            a = jnp.where(row == k, line, a - column * line)
    diagonal = jnp.sum(jnp.where(row == lane, a, 0.0), axis=1, keepdims=True)
    real = lax.rem(row, padded) < members
    w = jnp.where(real, a / diagonal, 0.0)
    mean = jnp.sum(w, axis=0, keepdims=True) / total
    unit = jnp.where(lane - size == row, 1.0, 0.0)
    out_ref[...] = unit + (w - mean) / math.sqrt(total - 1)


def combine_kernel(groups, padded, width, t_ref, *refs):
    ins, out_ref = refs[: 3 * groups], refs[3 * groups]
    members, _, rows, columns = out_ref.shape
    step = pl.program_id(0)
    last = pl.num_programs(0) - 1
    first = groups * padded

    @pl.when(step < last)
    def _():
        base = pl.multiple_of(step * width, LANES)
        for c in range(0, width, LANES):
            for q in range(3):
                total = [jnp.zeros((rows, LANES), f32) for _ in range(members)]
                for g in range(groups):
                    for i in range(members):
                        value = ins[q * groups + g][i, :, c : c + LANES]
                        for j in range(members):
                            total[j] = total[j] + t_ref[g * padded + i, first + j] * value
                for j in range(members):
                    out_ref[j, q, :, pl.ds(pl.multiple_of(base + c, LANES), LANES)] = total[j]

    @pl.when(step == last)
    def _():
        for j in range(members):
            out_ref[j, 1] = out_ref[j, 1] - courant * east(out_ref[j, 0])


def body(
    sample_collection,
    seabed_profile,
    gauge_grid_position,
    observed_values,
    error_scale,
    perturbation,
    inflation,
):
    members, _, rows, columns = sample_collection.shape
    bands, mems = lax.axis_size("band"), lax.axis_size("mem")
    total_rows, total = rows * bands, members * mems
    padded = pad8(members)
    first_row = lax.axis_index("band") * rows
    row_index = first_row.reshape(1)

    field = jax.ShapeDtypeStruct((members, rows, columns), f32)
    edge = jax.ShapeDtypeStruct((members, 1, columns), f32)
    whole = pl.BlockSpec((None, rows, columns), lambda m: (m, 0, 0))
    line = pl.BlockSpec((None, 1, columns), lambda m: (m, 0, 0))
    depth_spec = pl.BlockSpec((rows, columns), lambda m: (0, 0))
    smem = pl.BlockSpec(memory_space=pltpu.SMEM)
    size = 4 * members * rows * columns

    def part(q):
        return pl.BlockSpec((None, None, rows, columns), lambda m: (m, q, 0, 0))

    def height(h, u, v, above, below, specs, name):
        return pl.pallas_call(
            height_kernel,
            grid=(members,),
            in_specs=[*specs, depth_spec, line, line],
            out_specs=[whole, line, line],
            out_shape=[field, edge, edge],
            cost_estimate=cost(20 * size, 4 * size),
            name=name,
        )(h, u, v, seabed_profile, above, below)

    x = sample_collection
    low = x[:, 2, :1, :] * seabed_profile[:1]
    high = x[:, 2, rows - 1 :, :] * seabed_profile[rows - 1 :]
    above, below = shift_both(low, high)
    h, low, high = height(x, x, x, above, below, [part(0), part(1), part(2)], "height0")
    above, below = shift_both(low, high)
    u, v, w, low, high = pl.pallas_call(
        functools.partial(speed_kernel, total_rows),
        grid=(members,),
        in_specs=[smem, whole, part(1), part(2), depth_spec, line, line],
        out_specs=[whole, whole, whole, line, line],
        out_shape=[field, field, field, edge, edge],
        cost_estimate=cost(30 * size, 6 * size),
        name="speed0",
    )(row_index, h, x, x, seabed_profile, above, below)
    w_far = far_gather(w)
    above, below = shift_both(low, high)
    h, low, high = height(h, u, v, above, below, [whole] * 3, "height1")

    lines = gauge_grid_position.shape[0]
    cells = gauge_grid_position - first_row * columns
    predicted = pl.pallas_call(
        probe_kernel,
        in_specs=[smem, pl.BlockSpec(memory_space=pltpu.VMEM)],
        out_specs=pl.BlockSpec(memory_space=pltpu.VMEM),
        out_shape=jax.ShapeDtypeStruct((lines, padded, LANES), f32),
        scratch_shapes=[pltpu.VMEM((rows * columns // LANES, padded, LANES), f32)],
        cost_estimate=cost(size, size),
        name="probe",
    )(cells, h)
    gathered = mem_gather(predicted)
    n = len(gathered)
    height_rows = n * padded
    reach = -(-(height_rows + padded) // LANES) * LANES
    vmem = pl.BlockSpec(memory_space=pltpu.VMEM)
    partial = pl.pallas_call(
        functools.partial(gram_kernel, total, members),
        in_specs=[smem] + [vmem] * (3 + n),
        out_specs=vmem,
        out_shape=jax.ShapeDtypeStruct((height_rows, reach), f32),
        scratch_shapes=[
            pltpu.VMEM((height_rows, lines * LANES), f32),
            pltpu.VMEM((reach, lines * LANES), f32),
        ],
        cost_estimate=cost(1000000, 200000),
        name="gram",
    )(inflation, observed_values, error_scale, perturbation, *gathered)
    summed = band_sum(partial)
    transform = pl.pallas_call(
        functools.partial(solve_kernel, total, members, n),
        in_specs=[smem, vmem],
        out_specs=vmem,
        out_shape=jax.ShapeDtypeStruct((height_rows, reach), f32),
        cost_estimate=cost(1000000, 40000),
        name="solve",
    )(inflation, summed)

    h_far = far_gather(h)
    above, below = shift_both(low, high)
    v = pl.pallas_call(
        functools.partial(last_kernel, total_rows),
        grid=(members,),
        in_specs=[smem, whole, whole, whole, line, line],
        out_specs=whole,
        out_shape=field,
        cost_estimate=cost(20 * size, 4 * size),
        name="speed1",
    )(row_index, h, w, v, above, below)
    v_far = far_gather(v)

    pieces = []
    for own, far in ((h, h_far), (w, w_far), (v, v_far)):
        blocks = [own] + far
        if mems % 2 == 0:
            blocks = blocks + [near_swap(b) for b in blocks]
        pieces += blocks
    width = min(512, columns)
    steps = columns // width
    chunk = pl.BlockSpec((members, rows, width), lambda s: (0, 0, jnp.minimum(s, steps - 1)))
    return pl.pallas_call(
        functools.partial(combine_kernel, n, padded, width),
        grid=(steps + 1,),
        in_specs=[smem] + [chunk] * (3 * n),
        out_specs=pl.BlockSpec((members, 3, rows, columns), lambda s: (0, 0, 0, 0)),
        out_shape=jax.ShapeDtypeStruct((members, 3, rows, columns), f32),
        cost_estimate=cost(300 * size, 15 * size),
        name="combine",
    )(transform, *pieces)


def solution(mesh):
    in_specs = (
        P("mem", None, "band", None),
        P("band", None),
        P("band", None),
        P("band", None),
        P("band", None),
        P("mem", "band", None),
        P(),
    )
    out_specs = P("mem", None, "band", None)
    return jax.shard_map(body, mesh=mesh, in_specs=in_specs, out_specs=out_specs, check_vma=False)
```

```python
import functools
import math

import jax
import jax.numpy as jnp
from jax import lax
from jax.experimental import pallas as pl
from jax.experimental.pallas import tpu as pltpu
from jax.sharding import PartitionSpec as P


LANES = 128

courant = 0.5
coriolis_base = 0.15
coriolis_slope = 0.3


f32 = jnp.float32


def pad8(count):
    return -(-count // 8) * 8


def cost(flops, moved):
    return pl.CostEstimate(flops=flops, bytes_accessed=moved, transcendentals=0)


def shift_both(low_edge, high_edge):
    count = lax.axis_size("band")
    above = lax.ppermute(high_edge, "band", [(i, i + 1) for i in range(count - 1)])
    below = lax.ppermute(low_edge, "band", [(i + 1, i) for i in range(count - 1)])
    return above, below


def band_sum(part):
    count = lax.axis_size("band")
    if count & (count - 1):
        return lax.psum(part, "band")
    step = 1
    while step < count:
        other = lax.ppermute(part, "band", [(i, i ^ step) for i in range(count)])
        part = part + other
        step *= 2
    return part


def mem_plan(count):
    if count % 2 or count == 1:
        return [(s, None) for s in range(1, count)]
    far = [(2 * s, None) for s in range(1, count // 2)]
    return far


def far_gather(block):
    count = lax.axis_size("mem")
    return [
        lax.ppermute(block, "mem", [(i, (i + s) % count) for i in range(count)])
        for s, _ in mem_plan(count)
    ]


def near_swap(block):
    count = lax.axis_size("mem")
    return lax.ppermute(block, "mem", [(i, i ^ 1) for i in range(count)])


def east(q):
    columns = q.shape[-1]
    return (pltpu.roll(q, columns - 1, 1) - pltpu.roll(q, 1, 1)) * 0.5


def north(q, above, below):
    rows = q.shape[0]
    index = lax.broadcasted_iota(jnp.int32, q.shape, 0)
    up = jnp.where(index == rows - 1, below, pltpu.roll(q, rows - 1, 0))
    down = jnp.where(index == 0, above, pltpu.roll(q, 1, 0))
    return (up - down) * 0.5


def spin(first_row, shape, total_rows):
    rows = (first_row + lax.broadcasted_iota(jnp.int32, shape, 0)).astype(f32)
    return coriolis_base + coriolis_slope * (rows + 0.5) / total_rows


def edge_kernel(x_ref, b_ref, lo_out, hi_out):
    def member(m, _):
        flux = b_ref[...] * x_ref[m, 2]
        lo_out[m] = flux[:1]
        hi_out[m] = flux[-1:]
        return 0

    lax.fori_loop(0, x_ref.shape[0], member, 0)


def height_kernel(parts, h_ref, u_ref, v_ref, b_ref, above_ref, below_ref, h_out, lo_out, hi_out):
    depth = b_ref[...]

    def member(m, _):
        h0, u, v = (r[m] if q is None else r[m, q] for r, q in zip((h_ref, u_ref, v_ref), parts))
        h = h0 - courant * (east(depth * u) + north(depth * v, above_ref[m], below_ref[m]))
        h_out[m] = h
        lo_out[m] = h[:1]
        hi_out[m] = h[-1:]
        return 0

    lax.fori_loop(0, h_out.shape[0], member, 0)


def speed_kernel(
    total_rows, row_ref, h_ref, x_ref, b_ref, above_ref, below_ref,
    u_out, v_out, w_out, lo_out, hi_out,
):
    depth = b_ref[...]
    turn = spin(row_ref[0], depth.shape, total_rows)

    def member(m, _):
        h, v0 = h_ref[m], x_ref[m, 2]
        u = x_ref[m, 1] - courant * east(h) + turn * v0
        v = v0 - courant * north(h, above_ref[m], below_ref[m]) - turn * u
        u_out[m] = u
        v_out[m] = v
        w_out[m] = u + turn * v
        flux = depth * v
        lo_out[m] = flux[:1]
        hi_out[m] = flux[-1:]
        return 0

    lax.fori_loop(0, h_ref.shape[0], member, 0)


def last_kernel(total_rows, row_ref, h_ref, w_ref, v_ref, above_ref, below_ref, v_out):
    turn = spin(row_ref[0], h_ref.shape[1:], total_rows)

    def member(m, _):
        h = h_ref[m]
        u = w_ref[m] - courant * east(h)
        v_out[m] = v_ref[m] - courant * north(h, above_ref[m], below_ref[m]) - turn * u
        return 0

    lax.fori_loop(0, h_ref.shape[0], member, 0)


def probe_kernel(
    row_ref, cell_ref, h_ref, u_ref, v_ref, b_ref, above_ref, below_ref,
    h_out, lo_out, hi_out, out_ref, cells,
):
    members, rows, columns = h_ref.shape
    stride = rows * columns // LANES
    depth = b_ref[...]

    def member(m, _):
        h = h_ref[m] - courant * (
            east(depth * u_ref[m]) + north(depth * v_ref[m], above_ref[m], below_ref[m])
        )
        h_out[m] = h
        lo_out[m] = h[:1]
        hi_out[m] = h[-1:]
        base = pl.multiple_of(m * stride, 8)
        for c in range(columns // LANES):
            cells[pl.ds(base + c * rows, rows), :] = h[:, c * LANES : (c + 1) * LANES]
        return 0

    lax.fori_loop(0, members, member, 0)
    first = row_ref[0] * columns
    out_ref[...] = jnp.zeros_like(out_ref)
    lane = lax.broadcasted_iota(jnp.int32, (members, LANES), 1)
    for k in range(out_ref.shape[0]):

        def take(i, held, k=k):
            cell = cell_ref[k, i] - first
            row, column = cell // columns, lax.rem(cell, columns)
            start = (column // LANES) * rows + row
            piece = cells[pl.ds(start, members, stride=stride), :]
            turned = pltpu.roll(piece, lax.rem(i - lax.rem(column, LANES) + LANES, LANES), 1)
            return jnp.where(lane == i, turned, held)

        out_ref[k, :members, :] = lax.fori_loop(
            0, LANES, take, jnp.zeros((members, LANES), f32), unroll=8
        )


def gram_kernel(total, members, inf_ref, obs_ref, scale_ref, pert_ref, *refs):
    out_ref, spread, both = refs[-3:]
    groups = refs[:-3]
    padded = groups[0].shape[1]
    real = lax.broadcasted_iota(jnp.int32, (padded, LANES), 0) < members
    root = jnp.sqrt(jnp.full((1, LANES), inf_ref[0], f32))
    both[...] = jnp.zeros_like(both)
    for k in range(groups[0].shape[0]):
        at = slice(k * LANES, (k + 1) * LANES)
        scale = scale_ref[k : k + 1, :]
        sums = groups[0][k]
        for g in groups[1:]:
            sums = sums + g[k]
        centre = jnp.sum(sums, axis=0, keepdims=True) / total
        for n, g in enumerate(groups):
            s = jnp.where(real, (g[k] - centre) / (scale * math.sqrt(total - 1)), 0.0)
            spread[n * padded : (n + 1) * padded, at] = s
            both[n * padded : (n + 1) * padded, at] = s
        for m in range(members):
            both[len(groups) * padded + m : len(groups) * padded + m + 1, at] = (
                obs_ref[k : k + 1, :]
                + root * scale * pert_ref[m, k : k + 1, :]
                - groups[0][k, m : m + 1, :]
            ) / scale
    out_ref[...] = lax.dot_general(
        spread[...], both[...], (((1,), (1,)), ((), ())),
        precision=lax.Precision.HIGHEST, preferred_element_type=f32,
    )


def solve_kernel(total, members, groups, inf_ref, part_ref, out_ref):
    a = part_ref[...]
    size = a.shape[0]
    padded = size // groups
    row = lax.broadcasted_iota(jnp.int32, a.shape, 0)
    lane = lax.broadcasted_iota(jnp.int32, a.shape, 1)
    a = a + jnp.where(row == lane, inf_ref[0], 0.0)
    for g in range(groups):
        for m in range(members):
            k = g * padded + m
            pivot = a[k : k + 1, k : k + 1]
            inverse = 1.0 / jnp.sqrt(pivot)
            line = a[k : k + 1, :] * inverse
            column = a[:, k : k + 1] * inverse
            a = jnp.where(row == k, line, a - column * line)
    diagonal = jnp.sum(jnp.where(row == lane, a, 0.0), axis=1, keepdims=True)
    real = lax.rem(row, padded) < members
    w = jnp.where(real, a / diagonal, 0.0)
    mean = jnp.sum(w, axis=0, keepdims=True) / total
    unit = jnp.where(lane - size == row, 1.0, 0.0)
    out_ref[...] = unit + (w - mean) / math.sqrt(total - 1)


def weighted(t_ref, pieces, at, first, members, rows, width, start=None):
    total = list(start) if start is not None else [jnp.zeros((rows, width), f32)] * members
    for g, ref in pieces:
        for i in range(members):
            value = ref[i, :, at]
            for j in range(members):
                total[j] = total[j] + t_ref[g + i, first + j] * value
    return total


def blend_kernel(groups, padded, near, width, t_ref, *refs):
    ins, (out_ref, v_out, h_new, u_new, sems) = refs[:-5], refs[-5:]
    members, rows, columns = v_out.shape
    first = groups * padded
    heights = [(g * padded, r) for g, r in enumerate(ins[:groups])]
    speeds = [(g * padded, r) for g, r in enumerate(ins[groups : 2 * groups])]
    sides = [(g * padded, r) for g, r in zip(near, ins[2 * groups :])]

    def chunk(c, _):
        at = pl.ds(pl.multiple_of(c * width, LANES), width)
        for pieces, out in ((heights, h_new), (speeds, u_new), (sides, v_out)):
            for j, t in enumerate(weighted(t_ref, pieces, at, first, members, rows, width)):
                out[j, :, at] = t
        return 0

    lax.fori_loop(0, columns // width, chunk, 0)
    copies = [pltpu.make_async_copy(h_new, out_ref.at[:, 0], sems.at[0])]
    copies[0].start()

    def member(j, _):
        u_new[j] = u_new[j] - courant * east(h_new[j])
        return 0

    lax.fori_loop(0, members, member, 0)
    copies.append(pltpu.make_async_copy(u_new, out_ref.at[:, 1], sems.at[1]))
    copies[1].start()
    for copy in copies:
        copy.wait()


def finish_kernel(groups, padded, far, width, t_ref, part_ref, *refs):
    ins, (held_ref, out_ref, v_new, sems) = refs[:-4], refs[-4:]
    del held_ref
    members, rows, columns = part_ref.shape
    first = groups * padded
    sides = [(g * padded, r) for g, r in zip(far, ins)]
    copies = []
    for c in range(columns // width):
        at = pl.ds(c * width, width)
        start = [part_ref[j, :, at] for j in range(members)]
        for j, t in enumerate(weighted(t_ref, sides, at, first, members, rows, width, start)):
            v_new[j, :, at] = t
        copies.append(
            pltpu.make_async_copy(v_new.at[:, :, at], out_ref.at[:, 2, :, at], sems.at[c])
        )
        copies[-1].start()
    for copy in copies:
        copy.wait()


def body(
    sample_collection,
    seabed_profile,
    gauge_grid_position,
    observed_values,
    error_scale,
    perturbation,
    inflation,
):
    members, _, rows, columns = sample_collection.shape
    bands, mems = lax.axis_size("band"), lax.axis_size("mem")
    total_rows, total = rows * bands, members * mems
    padded = pad8(members)
    first_row = lax.axis_index("band") * rows
    row_index = first_row.reshape(1)

    field = jax.ShapeDtypeStruct((members, rows, columns), f32)
    edge = jax.ShapeDtypeStruct((members, 1, columns), f32)
    smem = pl.BlockSpec(memory_space=pltpu.SMEM)
    vmem = pl.BlockSpec(memory_space=pltpu.VMEM)
    hbm = pl.BlockSpec(memory_space=pl.ANY)
    size = 4 * members * rows * columns

    def call(kernel, ins, outs, shapes, limit, flops, moved, scratch=(), aliases={}):
        return pl.pallas_call(
            kernel,
            in_specs=ins,
            out_specs=outs,
            out_shape=shapes,
            scratch_shapes=list(scratch),
            input_output_aliases=aliases,
            compiler_params=pltpu.CompilerParams(vmem_limit_bytes=limit << 20),
            cost_estimate=cost(flops, moved),
        )

    x = sample_collection
    low, high = call(
        edge_kernel, [vmem] * 2, [vmem] * 2, [edge, edge], 6, size, size
    )(x, seabed_profile)
    above, below = shift_both(low, high)
    h, low, high = call(
        functools.partial(height_kernel, (0, 1, 2)),
        [vmem] * 6, [vmem] * 3, [field, edge, edge], 12, 20 * size, 4 * size,
    )(x, x, x, seabed_profile, above, below)
    above, below = shift_both(low, high)
    u, v, w, low, high = call(
        functools.partial(speed_kernel, total_rows),
        [smem] + [vmem] * 5, [vmem] * 5, [field, field, field, edge, edge], 12,
        30 * size, 6 * size,
    )(row_index, h, x, seabed_profile, above, below)
    above, below = shift_both(low, high)
    w_far = far_gather(w)

    lines = gauge_grid_position.shape[0]
    h, low, high, predicted = call(
        probe_kernel,
        [smem, smem] + [vmem] * 6, [vmem] * 4,
        [field, edge, edge, jax.ShapeDtypeStruct((lines, padded, LANES), f32)], 12,
        20 * size, 4 * size,
        scratch=[pltpu.VMEM((members * rows * columns // LANES, LANES), f32)],
    )(row_index, gauge_grid_position, h, u, v, seabed_profile, above, below)
    gathered = [predicted] + far_gather(predicted)
    if mems % 2 == 0:
        gathered = gathered + [near_swap(b) for b in gathered]
    n = len(gathered)
    height_rows = n * padded
    reach = -(-(height_rows + padded) // LANES) * LANES
    partial = call(
        functools.partial(gram_kernel, total, members),
        [smem] + [vmem] * (3 + n), vmem, jax.ShapeDtypeStruct((height_rows, reach), f32), 8,
        1000000, 200000,
        scratch=[
            pltpu.VMEM((height_rows, lines * LANES), f32),
            pltpu.VMEM((reach, lines * LANES), f32),
        ],
    )(inflation, observed_values, error_scale, perturbation, *gathered)
    summed = band_sum(partial)
    transform = call(
        functools.partial(solve_kernel, total, members, n),
        [smem, vmem], vmem, jax.ShapeDtypeStruct((height_rows, reach), f32), 4,
        1000000, 40000,
    )(inflation, summed)

    h_far = far_gather(h)
    above, below = shift_both(low, high)
    v = call(
        functools.partial(last_kernel, total_rows),
        [smem] + [vmem] * 5, vmem, field, 12, 20 * size, 4 * size,
    )(row_index, h, w, v, above, below)
    v_far = far_gather(v)

    def grouped(own, far):
        if mems % 2:
            return [own] + far
        own_near = near_swap(own)
        return [own] + far + [own_near] + [near_swap(b) for b in far]

    heights, speeds, sides = grouped(h, h_far), grouped(w, w_far), grouped(v, v_far)
    near = [0] if mems % 2 else [0, n // 2]
    far = [g for g in range(n) if g not in near]
    width = math.gcd(512, columns)
    whole = jax.ShapeDtypeStruct((members, 3, rows, columns), f32)
    out, v_part = call(
        functools.partial(blend_kernel, n, padded, near, width),
        [smem] + [vmem] * (2 * n + len(near)), [hbm, vmem], [whole, field], 4 + 2 * n,
        200 * size, 15 * size,
        scratch=[
            pltpu.VMEM((members, rows, columns), f32),
            pltpu.VMEM((members, rows, columns), f32),
            pltpu.SemaphoreType.DMA((2,)),
        ],
    )(transform, *heights, *speeds, *[sides[g] for g in near])
    return call(
        functools.partial(finish_kernel, n, padded, far, width),
        [smem] + [vmem] * (1 + len(far)) + [hbm], hbm, whole, 4 + n,
        100 * size, 5 * size,
        scratch=[
            pltpu.VMEM((members, rows, columns), f32),
            pltpu.SemaphoreType.DMA((columns // width,)),
        ],
        aliases={2 + len(far): 0},
    )(transform, v_part, *[sides[g] for g in far], out)


def solution(mesh):
    in_specs = (
        P("mem", None, "band", None),
        P("band", None),
        P("band", None),
        P("band", None),
        P("band", None),
        P("mem", "band", None),
        P(),
    )
    out_specs = P("mem", None, "band", None)

    return jax.shard_map(body, mesh=mesh, in_specs=in_specs, out_specs=out_specs, check_vma=False)
```

```python
import functools
import math

import jax
import jax.numpy as jnp
from jax import lax
from jax.experimental import pallas as pl
from jax.experimental.pallas import tpu as pltpu
from jax.sharding import PartitionSpec as P


LANES = 128

courant = 0.5
coriolis_base = 0.15
coriolis_slope = 0.3


f32 = jnp.float32


def pad8(count):
    return -(-count // 8) * 8


def cost(flops, moved):
    return pl.CostEstimate(flops=flops, bytes_accessed=moved, transcendentals=0)


def swap_edges(even, odd):
    count = lax.axis_size("band")

    def pairs(start):
        first = [(i, i + 1) for i in range(start, count - 1, 2)]
        return first + [(j, i) for i, j in first]

    even = lax.ppermute(even, "band", pairs(0))
    odd = lax.ppermute(odd, "band", pairs(1))
    return even, odd


def pick(row_ref, rows, top, bottom):
    odd = lax.rem(lax.div(row_ref[0], rows), 2) == 1
    return jnp.where(odd, top, bottom), jnp.where(odd, bottom, top)


def band_sum(part):
    count = lax.axis_size("band")
    if count & (count - 1):
        return lax.psum(part, "band")
    step = 1
    while step < count:
        other = lax.ppermute(part, "band", [(i, i ^ step) for i in range(count)])
        part = part + other
        step *= 2
    return part


def mem_plan(count):
    if count % 2 or count == 1:
        return [(s, None) for s in range(1, count)]
    far = [(2 * s, None) for s in range(1, count // 2)]
    return far


def far_gather(block):
    count = lax.axis_size("mem")
    return [
        lax.ppermute(block, "mem", [(i, (i + s) % count) for i in range(count)])
        for s, _ in mem_plan(count)
    ]


def near_swap(block):
    count = lax.axis_size("mem")
    return lax.ppermute(block, "mem", [(i, i ^ 1) for i in range(count)])


def east(q):
    columns = q.shape[-1]
    return (pltpu.roll(q, columns - 1, 1) - pltpu.roll(q, 1, 1)) * 0.5


def north(q, above, below):
    rows = q.shape[0]
    index = lax.broadcasted_iota(jnp.int32, q.shape, 0)
    up = jnp.where(index == rows - 1, below, pltpu.roll(q, rows - 1, 0))
    down = jnp.where(index == 0, above, pltpu.roll(q, 1, 0))
    return (up - down) * 0.5


def spin(first_row, shape, total_rows):
    rows = (first_row + lax.broadcasted_iota(jnp.int32, shape, 0)).astype(f32)
    return coriolis_base + coriolis_slope * (rows + 0.5) / total_rows


def edge_kernel(row_ref, x_ref, b_ref, even_out, odd_out, speed, depth, sems):
    copies = [
        pltpu.make_async_copy(b_ref, depth, sems.at[0]),
        pltpu.make_async_copy(x_ref.at[:, 2], speed, sems.at[1]),
    ]
    for copy in copies:
        copy.start()
    for copy in copies:
        copy.wait()

    def member(m, _):
        flux = depth[...] * speed[m]
        even_out[m], odd_out[m] = pick(row_ref, depth.shape[0], flux[:1], flux[-1:])
        return 0

    lax.fori_loop(0, x_ref.shape[0], member, 0)


def height_kernel(
    total_rows, row_ref, x_ref, b_ref, even_ref, odd_ref, h_out, u_out, even_out, odd_out
):
    depth = b_ref[...]
    rows = depth.shape[0]
    turn = spin(row_ref[0], depth.shape, total_rows)

    def member(m, _):
        u, v = x_ref[m, 1], x_ref[m, 2]
        above, below = pick(row_ref, rows, even_ref[m], odd_ref[m])
        h = x_ref[m, 0] - courant * (east(depth * u) + north(depth * v, above, below))
        h_out[m] = h
        u_out[m] = u - courant * east(h) + turn * v
        even_out[m], odd_out[m] = pick(row_ref, rows, h[:1], h[-1:])
        return 0

    lax.fori_loop(0, h_out.shape[0], member, 0)


def speed_kernel(
    total_rows, row_ref, h_ref, u_ref, x_ref, b_ref, even_ref, odd_ref, even_out, odd_out, *v_outs
):
    depth = b_ref[...]
    rows = depth.shape[0]
    turn = spin(row_ref[0], depth.shape, total_rows)
    base = 0
    for v_out in v_outs:

        def member(i, _, v_out=v_out, base=base):
            m = base + i
            above, below = pick(row_ref, rows, even_ref[m], odd_ref[m])
            v = x_ref[m, 2] - courant * north(h_ref[m], above, below) - turn * u_ref[m]
            v_out[i] = v
            flux = depth * v
            even_out[m], odd_out[m] = pick(row_ref, rows, flux[:1], flux[-1:])
            return 0

        lax.fori_loop(0, v_out.shape[0], member, 0)
        base += v_out.shape[0]


def split(value, by):
    if by & (by - 1):
        return lax.div(value, by), lax.rem(value, by)
    return lax.shift_right_logical(value, by.bit_length() - 1), value & (by - 1)


def probe_kernel(row_ref, code_ref, h_ref, u_ref, b_ref, even_ref, odd_ref, *refs):
    v_refs, (h_out, even_out, odd_out, out_ref, cells) = refs[:-5], refs[-5:]
    members, rows, columns = h_ref.shape
    stride = rows * columns // LANES
    depth = b_ref[...]
    offset = 0
    for v_ref in v_refs:

        def member(i, _, v_ref=v_ref, offset=offset):
            m = offset + i
            above, below = pick(row_ref, rows, even_ref[m], odd_ref[m])
            h = h_ref[m] - courant * (
                east(depth * u_ref[m]) + north(depth * v_ref[i], above, below)
            )
            h_out[m] = h
            even_out[m], odd_out[m] = pick(row_ref, rows, h[:1], h[-1:])
            base = pl.multiple_of(m * stride, 8)
            for c in range(columns // LANES):
                cells[pl.ds(base + c * rows, rows), :] = h[:, c * LANES : (c + 1) * LANES]
            return 0

        lax.fori_loop(0, v_ref.shape[0], member, 0)
        offset += v_ref.shape[0]
    out_ref[...] = jnp.zeros_like(out_ref)
    lane = lax.broadcasted_iota(jnp.int32, (members, LANES), 1)
    for k in range(out_ref.shape[0]):

        def take(i, held, k=k):
            start, turn = split(code_ref[k, i], LANES)
            piece = cells[pl.ds(start, members, stride=stride), :]
            turned = pltpu.roll(piece, turn, 1)
            return jnp.where(lane == i, turned, held)

        out_ref[k, :members, :] = lax.fori_loop(
            0, LANES, take, jnp.zeros((members, LANES), f32), unroll=16
        )


def pack_kernel(rows, row_ref, even_ref, odd_ref, out_ref):
    width = out_ref.shape[-1]

    def member(m, _):
        for side, line in enumerate(pick(row_ref, rows, even_ref[m], odd_ref[m])):
            for s in range(8):
                out_ref[m, side, s : s + 1, :] = line[:, s * width : (s + 1) * width]
        return 0

    lax.fori_loop(0, out_ref.shape[0], member, 0)


def gram_kernel(total, members, inf_ref, obs_ref, scale_ref, pert_ref, *refs):
    out_ref, spread, both = refs[-3:]
    groups = refs[:-3]
    padded = groups[0].shape[1]
    real = lax.broadcasted_iota(jnp.int32, (padded, LANES), 0) < members
    root = jnp.sqrt(jnp.full((1, LANES), inf_ref[0], f32))
    both[...] = jnp.zeros_like(both)
    for k in range(groups[0].shape[0]):
        at = slice(k * LANES, (k + 1) * LANES)
        scale = scale_ref[k : k + 1, :]
        sums = groups[0][k]
        for g in groups[1:]:
            sums = sums + g[k]
        centre = jnp.sum(sums, axis=0, keepdims=True) / total
        for n, g in enumerate(groups):
            s = jnp.where(real, (g[k] - centre) / (scale * math.sqrt(total - 1)), 0.0)
            spread[n * padded : (n + 1) * padded, at] = s
            both[n * padded : (n + 1) * padded, at] = s
        for m in range(members):
            both[len(groups) * padded + m : len(groups) * padded + m + 1, at] = (
                obs_ref[k : k + 1, :]
                + root * scale * pert_ref[m, k : k + 1, :]
                - groups[0][k, m : m + 1, :]
            ) / scale
    out_ref[...] = lax.dot_general(
        spread[...], both[...], (((1,), (1,)), ((), ())),
        precision=lax.Precision.HIGHEST, preferred_element_type=f32,
    )


def solve_kernel(total, members, groups, inf_ref, part_ref, out_ref):
    a = part_ref[...]
    size = a.shape[0]
    padded = size // groups
    row = lax.broadcasted_iota(jnp.int32, a.shape, 0)
    lane = lax.broadcasted_iota(jnp.int32, a.shape, 1)
    a = a + jnp.where(row == lane, inf_ref[0], 0.0)
    for g in range(groups):
        for m in range(members):
            k = g * padded + m
            pivot = a[k : k + 1, k : k + 1]
            inverse = 1.0 / jnp.sqrt(pivot)
            line = a[k : k + 1, :] * inverse
            column = a[:, k : k + 1] * inverse
            a = jnp.where(row == k, line, a - column * line)
    diagonal = jnp.sum(jnp.where(row == lane, a, 0.0), axis=1, keepdims=True)
    real = lax.rem(row, padded) < members
    w = jnp.where(real, a / diagonal, 0.0)
    mean = jnp.sum(w, axis=0, keepdims=True) / total
    unit = jnp.where(lane - size == row, 1.0, 0.0)
    out_ref[...] = unit + (w - mean) / math.sqrt(total - 1)


def weighted(t_ref, pieces, at, first, members, rows, width, start=None):
    total = list(start) if start is not None else [jnp.zeros((rows, width), f32)] * members
    for g, ref in pieces:
        for i in range(ref.shape[0]):
            value = ref[i, :, at]
            for j in range(members):
                total[j] = total[j] + t_ref[g + i, first + j] * value
    return total


def blend_kernel(lists, first, width, t_ref, *refs):
    outs = refs[-len(lists) :]
    members, rows, columns = outs[0].shape

    def chunk(c, _):
        at = pl.ds(pl.multiple_of(c * width, LANES), width)
        start = 0
        for places, out in zip(lists, outs):
            pieces = list(zip(places, refs[start:]))
            start += len(places)
            for j, t in enumerate(weighted(t_ref, pieces, at, first, members, rows, width)):
                out[j, :, at] = t
        return 0

    lax.fori_loop(0, columns // width, chunk, 0)


def settle_kernel(places, first, width, t_ref, part_ref, *refs):
    pieces = list(zip(places, refs))
    h_out = refs[len(places)]
    members, rows, columns = part_ref.shape

    def chunk(c, _):
        at = pl.ds(pl.multiple_of(c * width, LANES), width)
        start = [part_ref[j, :, at] for j in range(members)]
        for j, t in enumerate(weighted(t_ref, pieces, at, first, members, rows, width, start)):
            h_out[j, :, at] = t
        return 0

    lax.fori_loop(0, columns // width, chunk, 0)


def turn_kernel(total_rows, row_ref, h_ref, u_ref, v_ref, out_ref, v_out, u_new, sems):
    copies = [pltpu.make_async_copy(h_ref, out_ref.at[:, 0], sems.at[0])]
    copies[0].start()
    members, rows, columns = h_ref.shape
    turn = spin(row_ref[0], (rows, columns), total_rows)

    def eastward(j, _):
        u_new[j] = u_ref[j] - courant * east(h_ref[j]) + turn * v_ref[j]
        return 0

    lax.fori_loop(0, members, eastward, 0)
    copies.append(pltpu.make_async_copy(u_new, out_ref.at[:, 1], sems.at[1]))
    copies[1].start()

    def northward(j, _):
        v_out[j] = v_ref[j] - courant * north(h_ref[j], 0.0, 0.0) - turn * u_new[j]
        return 0

    lax.fori_loop(0, members, northward, 0)
    for copy in copies:
        copy.wait()


def finish_kernel(places, first, t_ref, part_ref, *refs):
    ins, (held_ref, out_ref, v_new, sems) = refs[:-4], refs[-4:]
    del held_ref
    members, rows, columns = part_ref.shape
    width = columns // 8
    copies = []
    totals = []
    for side in range(2):
        total = [jnp.zeros((8, width), f32)] * members
        for g, ref in zip(places, ins):
            for i in range(members):
                value = ref[i, side]
                for j in range(members):
                    total[j] = total[j] + t_ref[g + i, first + j] * value
        totals.append(total)
    for j in range(members):
        v_new[j] = part_ref[j]
        for s in range(8):
            at = slice(s * width, (s + 1) * width)
            v_new[j, :1, at] = v_new[j, :1, at] + (courant * 0.5) * totals[0][j][s : s + 1]
            v_new[j, rows - 1 :, at] = (
                v_new[j, rows - 1 :, at] - (courant * 0.5) * totals[1][j][s : s + 1]
            )
        copies.append(pltpu.make_async_copy(v_new.at[j], out_ref.at[j, 2], sems.at[j]))
        copies[-1].start()
    for copy in copies:
        copy.wait()


def body(
    sample_collection,
    seabed_profile,
    gauge_grid_position,
    observed_values,
    error_scale,
    perturbation,
    inflation,
):
    members, _, rows, columns = sample_collection.shape
    bands, mems = lax.axis_size("band"), lax.axis_size("mem")
    total_rows, total = rows * bands, members * mems
    padded = pad8(members)
    first_row = lax.axis_index("band") * rows
    row_index = first_row.reshape(1)

    field = jax.ShapeDtypeStruct((members, rows, columns), f32)
    edge = jax.ShapeDtypeStruct((members, 1, columns), f32)
    smem = pl.BlockSpec(memory_space=pltpu.SMEM)
    vmem = pl.BlockSpec(memory_space=pltpu.VMEM)
    hbm = pl.BlockSpec(memory_space=pl.ANY)
    size = 4 * members * rows * columns

    def call(kernel, ins, outs, shapes, limit, flops, moved, scratch=(), aliases={}):
        return pl.pallas_call(
            kernel,
            in_specs=ins,
            out_specs=outs,
            out_shape=shapes,
            scratch_shapes=list(scratch),
            input_output_aliases=aliases,
            compiler_params=pltpu.CompilerParams(vmem_limit_bytes=limit << 20),
            cost_estimate=cost(flops, moved),
        )

    x = sample_collection
    early = -(-2 * members // 3)
    halves = [count for count in (early, members - early) if count]
    fields = [jax.ShapeDtypeStruct((count, rows, columns), f32) for count in halves]
    even, odd = call(
        edge_kernel, [smem, hbm, hbm], [vmem] * 2, [edge, edge], 60, size, size,
        scratch=[
            pltpu.VMEM((members, rows, columns), f32),
            pltpu.VMEM((rows, columns), f32),
            pltpu.SemaphoreType.DMA((2,)),
        ],
    )(row_index, x, seabed_profile)
    even, odd = swap_edges(even, odd)
    h, u, even, odd = call(
        functools.partial(height_kernel, total_rows),
        [smem] + [vmem] * 4, [vmem] * 4, [field, field, edge, edge], 12, 20 * size, 4 * size,
    )(row_index, x, seabed_profile, even, odd)
    u_far = far_gather(u)
    even, odd = swap_edges(even, odd)
    even, odd, *v = call(
        functools.partial(speed_kernel, total_rows),
        [smem] + [vmem] * 6, [vmem] * (2 + len(halves)), [edge, edge, *fields], 12,
        30 * size, 6 * size,
    )(row_index, h, u, x, seabed_profile, even, odd)
    v_far = []
    for block in v:
        v_far.append(far_gather(block))
    even, odd = swap_edges(even, odd)

    lines = gauge_grid_position.shape[0]
    cell = gauge_grid_position - first_row * columns
    row, column = split(cell, columns)
    block, place = split(column, LANES)
    lane = lax.broadcasted_iota(jnp.int32, cell.shape, 1)
    code = (block * rows + row) * LANES + ((lane - place) & (LANES - 1))
    h, even, odd, predicted = call(
        probe_kernel,
        [smem, smem] + [vmem] * (5 + len(v)), [vmem] * 4,
        [field, edge, edge, jax.ShapeDtypeStruct((lines, padded, LANES), f32)], 12,
        20 * size, 4 * size,
        scratch=[pltpu.VMEM((members * rows * columns // LANES, LANES), f32)],
    )(row_index, code, h, u, seabed_profile, even, odd, *v)
    gathered = [predicted] + far_gather(predicted)
    if mems % 2 == 0:
        gathered = gathered + [near_swap(b) for b in gathered]
    n = len(gathered)
    height_rows = n * padded
    reach = -(-(height_rows + padded) // LANES) * LANES
    partial = call(
        functools.partial(gram_kernel, total, members),
        [smem] + [vmem] * (3 + n), vmem, jax.ShapeDtypeStruct((height_rows, reach), f32), 8,
        1000000, 200000,
        scratch=[
            pltpu.VMEM((height_rows, lines * LANES), f32),
            pltpu.VMEM((reach, lines * LANES), f32),
        ],
    )(inflation, observed_values, error_scale, perturbation, *gathered)
    summed = band_sum(partial)
    transform = call(
        functools.partial(solve_kernel, total, members, n),
        [smem, vmem], vmem, jax.ShapeDtypeStruct((height_rows, reach), f32), 4,
        1000000, 40000,
    )(inflation, summed)

    h_far = far_gather(h)
    even, odd = swap_edges(even, odd)
    rim = call(
        functools.partial(pack_kernel, rows), [smem] + [vmem] * 2, vmem,
        jax.ShapeDtypeStruct((members, 2, 8, columns // 8), f32), 4, size // 4, size // 2,
    )(row_index, even, odd)
    rim_far = far_gather(rim)

    def grouped(own, far):
        if mems % 2:
            return [own] + far
        own_near = near_swap(own)
        return [own] + far + [own_near] + [near_swap(b) for b in far]

    speeds, heights, rims = grouped(u, u_far), grouped(h, h_far), grouped(rim, rim_far)
    sides = [grouped(b, f) for b, f in zip(v, v_far)]
    every = [g * padded for g in range(n)]
    near = [0] if mems % 2 else [0, n // 2]
    far = [g for g in range(n) if g not in near]
    side_places, begin = [], 0
    for count in halves:
        side_places += [g + begin for g in every]
        begin += count
    width = math.gcd(512, columns)
    whole = jax.ShapeDtypeStruct((members, 3, rows, columns), f32)

    def blend(lists, blocks):
        return call(
            functools.partial(blend_kernel, lists, height_rows, width),
            [smem] + [vmem] * len(blocks), [vmem] * len(lists), [field] * len(lists),
            4 + 2 * n, 100 * size, 10 * size,
        )(transform, *blocks)

    u_sum, h_part = blend((every, [every[g] for g in near]), [*speeds, *(heights[g] for g in near)])
    (v_sum,) = blend((side_places,), [b for side in sides for b in side])
    h_new = call(
        functools.partial(settle_kernel, [every[g] for g in far], height_rows, width),
        [smem] + [vmem] * (1 + len(far)), vmem, field, 6 + n, 50 * size, 4 * size,
    )(transform, h_part, *(heights[g] for g in far))
    out, v_part = call(
        functools.partial(turn_kernel, total_rows),
        [smem] + [vmem] * 3, [hbm, vmem], [whole, field], 8, 20 * size, 6 * size,
        scratch=[pltpu.VMEM((members, rows, columns), f32), pltpu.SemaphoreType.DMA((2,))],
    )(row_index, h_new, u_sum, v_sum)
    return call(
        functools.partial(finish_kernel, every, height_rows),
        [smem] + [vmem] * (1 + n) + [hbm], hbm, whole, 4 + n,
        20 * size, 3 * size,
        scratch=[
            pltpu.VMEM((members, rows, columns), f32),
            pltpu.SemaphoreType.DMA((members,)),
        ],
        aliases={2 + n: 0},
    )(transform, v_part, *rims, out)


def solution(mesh):
    in_specs = (
        P("mem", None, "band", None),
        P("band", None),
        P("band", None),
        P("band", None),
        P("band", None),
        P("mem", "band", None),
        P(),
    )
    out_specs = P("mem", None, "band", None)

    return jax.shard_map(body, mesh=mesh, in_specs=in_specs, out_specs=out_specs, check_vma=False)
```

```python
import functools
import math

import jax
import jax.numpy as jnp
from jax import lax
from jax.experimental import pallas as pl
from jax.experimental.pallas import tpu as pltpu
from jax.sharding import PartitionSpec as P


LANES = 128

courant = 0.5
coriolis_base = 0.15
coriolis_slope = 0.3


f32 = jnp.float32


def pad8(count):
    return -(-count // 8) * 8


def cost(flops, moved):
    return pl.CostEstimate(flops=flops, bytes_accessed=moved, transcendentals=0)


def swap_edges(even, odd):
    count = lax.axis_size("band")

    def pairs(start):
        first = [(i, i + 1) for i in range(start, count - 1, 2)]
        return first + [(j, i) for i, j in first]

    even = lax.ppermute(even, "band", pairs(0))
    odd = lax.ppermute(odd, "band", pairs(1))
    return even, odd


def pick(row_ref, rows, top, bottom):
    odd = lax.rem(lax.div(row_ref[0], rows), 2) == 1
    return jnp.where(odd, top, bottom), jnp.where(odd, bottom, top)


def band_sum(part):
    count = lax.axis_size("band")
    if count & (count - 1):
        return lax.psum(part, "band")
    step = 1
    while step < count:
        other = lax.ppermute(part, "band", [(i, i ^ step) for i in range(count)])
        part = part + other
        step *= 2
    return part


def mem_plan(count):
    if count % 2 or count == 1:
        return [(s, None) for s in range(1, count)]
    far = [(2 * s, None) for s in range(1, count // 2)]
    return far


def far_gather(block):
    count = lax.axis_size("mem")
    return [
        lax.ppermute(block, "mem", [(i, (i + s) % count) for i in range(count)])
        for s, _ in mem_plan(count)
    ]


def near_swap(block):
    count = lax.axis_size("mem")
    return lax.ppermute(block, "mem", [(i, i ^ 1) for i in range(count)])


def east(q):
    columns = q.shape[-1]
    return (pltpu.roll(q, columns - 1, 1) - pltpu.roll(q, 1, 1)) * 0.5


def north(q, above, below):
    rows = q.shape[0]
    index = lax.broadcasted_iota(jnp.int32, q.shape, 0)
    up = jnp.where(index == rows - 1, below, pltpu.roll(q, rows - 1, 0))
    down = jnp.where(index == 0, above, pltpu.roll(q, 1, 0))
    return (up - down) * 0.5


def spin(first_row, shape, total_rows):
    rows = (first_row + lax.broadcasted_iota(jnp.int32, shape, 0)).astype(f32)
    return coriolis_base + coriolis_slope * (rows + 0.5) / total_rows


def edge_kernel(row_ref, x_ref, b_ref, even_out, odd_out, speed, depth, sems):
    copies = [
        pltpu.make_async_copy(b_ref, depth, sems.at[0]),
        pltpu.make_async_copy(x_ref.at[:, 2], speed, sems.at[1]),
    ]
    for copy in copies:
        copy.start()
    for copy in copies:
        copy.wait()

    def member(m, _):
        flux = depth[...] * speed[m]
        even_out[m], odd_out[m] = pick(row_ref, depth.shape[0], flux[:1], flux[-1:])
        return 0

    lax.fori_loop(0, x_ref.shape[0], member, 0)


def index_kernel(rows, columns, row_ref, cell_ref, code_ref):
    row, column = split(cell_ref[...] - row_ref[0] * columns, columns)
    block, place = split(column, LANES)
    lane = lax.broadcasted_iota(jnp.int32, cell_ref.shape, 1)
    code_ref[...] = (block * rows + row) * LANES + ((lane - place) & (LANES - 1))


def begin_kernel(total_rows, row_ref, x_ref, b_ref, h_out, u_out):
    depth = b_ref[...]
    turn = spin(row_ref[0], depth.shape, total_rows)

    def member(m, _):
        u, v = x_ref[m, 1], x_ref[m, 2]
        h = x_ref[m, 0] - courant * (east(depth * u) + north(depth * v, 0.0, 0.0))
        h_out[m] = h
        u_out[m] = u - courant * east(h) + turn * v
        return 0

    lax.fori_loop(0, h_out.shape[0], member, 0)


def rim_rows(row_ref, shape, even, odd):
    rows = shape[0]
    above, below = pick(row_ref, rows, even, odd)
    index = lax.broadcasted_iota(jnp.int32, shape, 0)
    rim = jnp.where(index == 0, above, jnp.where(index == rows - 1, -below, 0.0))
    return (courant * 0.5) * rim


def height_kernel(
    row_ref, h_ref, u_ref, even_ref, odd_ref, h_out, u_out, even_out, odd_out
):
    rows = h_ref.shape[1]

    def member(m, _):
        rim = rim_rows(row_ref, h_ref.shape[1:], even_ref[m], odd_ref[m])
        h = h_ref[m] + rim
        h_out[m] = h
        even_out[m], odd_out[m] = pick(row_ref, rows, h[:1], h[-1:])
        u_out[m] = u_ref[m] - courant * east(rim)
        return 0

    lax.fori_loop(0, h_out.shape[0], member, 0)


def speed_kernel(
    total_rows, row_ref, h_ref, u_ref, x_ref, b_ref, even_ref, odd_ref, even_out, odd_out, *v_outs
):
    depth = b_ref[...]
    rows = depth.shape[0]
    turn = spin(row_ref[0], depth.shape, total_rows)
    base = 0
    for v_out in v_outs:

        def member(i, _, v_out=v_out, base=base):
            m = base + i
            above, below = pick(row_ref, rows, even_ref[m], odd_ref[m])
            v = x_ref[m, 2] - courant * north(h_ref[m], above, below) - turn * u_ref[m]
            v_out[i] = v
            flux = depth * v
            even_out[m], odd_out[m] = pick(row_ref, rows, flux[:1], flux[-1:])
            return 0

        lax.fori_loop(0, v_out.shape[0], member, 0)
        base += v_out.shape[0]


def split(value, by):
    if by & (by - 1):
        return lax.div(value, by), lax.rem(value, by)
    return lax.shift_right_logical(value, by.bit_length() - 1), value & (by - 1)


def third_kernel(h_ref, u_ref, b_ref, *refs):
    v_refs, h_out = refs[:-1], refs[-1]
    depth = b_ref[...]
    offset = 0
    for v_ref in v_refs:

        def member(i, _, v_ref=v_ref, offset=offset):
            m = offset + i
            h_out[m] = h_ref[m] - courant * (
                east(depth * u_ref[m]) + north(depth * v_ref[i], 0.0, 0.0)
            )
            return 0

        lax.fori_loop(0, v_ref.shape[0], member, 0)
        offset += v_ref.shape[0]


def probe_kernel(
    row_ref, code_ref, part_ref, even_ref, odd_ref, h_out, even_out, odd_out, out_ref, cells
):
    members, rows, columns = part_ref.shape
    stride = rows * columns // LANES

    def member(m, _):
        h = part_ref[m] + rim_rows(row_ref, (rows, columns), even_ref[m], odd_ref[m])
        h_out[m] = h
        even_out[m], odd_out[m] = pick(row_ref, rows, h[:1], h[-1:])
        base = pl.multiple_of(m * stride, 8)
        for c in range(columns // LANES):
            cells[pl.ds(base + c * rows, rows), :] = h[:, c * LANES : (c + 1) * LANES]
        return 0

    lax.fori_loop(0, members, member, 0)
    out_ref[...] = jnp.zeros_like(out_ref)
    lane = lax.broadcasted_iota(jnp.int32, (members, LANES), 1)
    for k in range(out_ref.shape[0]):

        def take(i, held, k=k):
            start, turn = split(code_ref[k, i], LANES)
            piece = cells[pl.ds(start, members, stride=stride), :]
            turned = pltpu.roll(piece, turn, 1)
            return jnp.where(lane == i, turned, held)

        out_ref[k, :members, :] = lax.fori_loop(
            0, LANES, take, jnp.zeros((members, LANES), f32), unroll=16
        )


def pack_kernel(rows, row_ref, even_ref, odd_ref, out_ref):
    width = out_ref.shape[-1]

    def member(m, _):
        for side, line in enumerate(pick(row_ref, rows, even_ref[m], odd_ref[m])):
            for s in range(8):
                out_ref[m, side, s : s + 1, :] = line[:, s * width : (s + 1) * width]
        return 0

    lax.fori_loop(0, out_ref.shape[0], member, 0)


def gram_kernel(total, members, inf_ref, obs_ref, scale_ref, pert_ref, *refs):
    out_ref, spread, both = refs[-3:]
    groups = refs[:-3]
    padded = groups[0].shape[1]
    real = lax.broadcasted_iota(jnp.int32, (padded, LANES), 0) < members
    root = jnp.sqrt(jnp.full((1, LANES), inf_ref[0], f32))
    both[...] = jnp.zeros_like(both)
    for k in range(groups[0].shape[0]):
        at = slice(k * LANES, (k + 1) * LANES)
        scale = scale_ref[k : k + 1, :]
        sums = groups[0][k]
        for g in groups[1:]:
            sums = sums + g[k]
        centre = jnp.sum(sums, axis=0, keepdims=True) / total
        for n, g in enumerate(groups):
            s = jnp.where(real, (g[k] - centre) / (scale * math.sqrt(total - 1)), 0.0)
            spread[n * padded : (n + 1) * padded, at] = s
            both[n * padded : (n + 1) * padded, at] = s
        for m in range(members):
            both[len(groups) * padded + m : len(groups) * padded + m + 1, at] = (
                obs_ref[k : k + 1, :]
                + root * scale * pert_ref[m, k : k + 1, :]
                - groups[0][k, m : m + 1, :]
            ) / scale
    out_ref[...] = lax.dot_general(
        spread[...], both[...], (((1,), (1,)), ((), ())),
        precision=lax.Precision.HIGHEST, preferred_element_type=f32,
    )


def solve_kernel(total, members, groups, inf_ref, part_ref, out_ref):
    a = part_ref[...]
    size = a.shape[0]
    padded = size // groups
    row = lax.broadcasted_iota(jnp.int32, a.shape, 0)
    lane = lax.broadcasted_iota(jnp.int32, a.shape, 1)
    a = a + jnp.where(row == lane, inf_ref[0], 0.0)
    for g in range(groups):
        for m in range(members):
            k = g * padded + m
            pivot = a[k : k + 1, k : k + 1]
            inverse = 1.0 / jnp.sqrt(pivot)
            line = a[k : k + 1, :] * inverse
            column = a[:, k : k + 1] * inverse
            a = jnp.where(row == k, line, a - column * line)
    diagonal = jnp.sum(jnp.where(row == lane, a, 0.0), axis=1, keepdims=True)
    real = lax.rem(row, padded) < members
    w = jnp.where(real, a / diagonal, 0.0)
    mean = jnp.sum(w, axis=0, keepdims=True) / total
    unit = jnp.where(lane - size == row, 1.0, 0.0)
    out_ref[...] = unit + (w - mean) / math.sqrt(total - 1)


def weighted(t_ref, pieces, at, first, members, rows, width, start=None):
    total = list(start) if start is not None else [jnp.zeros((rows, width), f32)] * members
    for g, ref in pieces:
        for i in range(ref.shape[0]):
            value = ref[i, :, at]
            for j in range(members):
                total[j] = total[j] + t_ref[g + i, first + j] * value
    return total


def blend_kernel(lists, first, width, t_ref, *refs):
    outs = refs[-len(lists) :]
    members, rows, columns = outs[0].shape

    def chunk(c, _):
        at = pl.ds(pl.multiple_of(c * width, LANES), width)
        start = 0
        for places, out in zip(lists, outs):
            pieces = list(zip(places, refs[start:]))
            start += len(places)
            for j, t in enumerate(weighted(t_ref, pieces, at, first, members, rows, width)):
                out[j, :, at] = t
        return 0

    lax.fori_loop(0, columns // width, chunk, 0)


def settle_kernel(places, first, width, t_ref, part_ref, *refs):
    pieces = list(zip(places, refs))
    h_out = refs[len(places)]
    members, rows, columns = part_ref.shape

    def chunk(c, _):
        at = pl.ds(pl.multiple_of(c * width, LANES), width)
        start = [part_ref[j, :, at] for j in range(members)]
        for j, t in enumerate(weighted(t_ref, pieces, at, first, members, rows, width, start)):
            h_out[j, :, at] = t
        return 0

    lax.fori_loop(0, columns // width, chunk, 0)


def turn_kernel(total_rows, row_ref, h_ref, u_ref, v_ref, u_out, v_out):
    members, rows, columns = h_ref.shape
    turn = spin(row_ref[0], (rows, columns), total_rows)

    def member(j, _):
        h, v = h_ref[j], v_ref[j]
        u = u_ref[j] - courant * east(h) + turn * v
        u_out[j] = u
        v_out[j] = v - courant * north(h, 0.0, 0.0) - turn * u
        return 0

    lax.fori_loop(0, members, member, 0)


def finish_kernel(places, first, t_ref, part_ref, h_ref, u_ref, *refs):
    ins, (out_ref, v_new, sems) = refs[:-3], refs[-3:]
    members, rows, columns = part_ref.shape
    width = columns // 8
    copies = [
        pltpu.make_async_copy(h_ref, out_ref.at[:, 0], sems.at[members]),
        pltpu.make_async_copy(u_ref, out_ref.at[:, 1], sems.at[members + 1]),
    ]
    for copy in copies:
        copy.start()
    totals = []
    for side in range(2):
        total = [jnp.zeros((8, width), f32)] * members
        for g, ref in zip(places, ins):
            for i in range(members):
                value = ref[i, side]
                for j in range(members):
                    total[j] = total[j] + t_ref[g + i, first + j] * value
        totals.append(total)
    for j in range(members):
        v_new[j] = part_ref[j]
        for s in range(8):
            at = slice(s * width, (s + 1) * width)
            v_new[j, :1, at] = v_new[j, :1, at] + (courant * 0.5) * totals[0][j][s : s + 1]
            v_new[j, rows - 1 :, at] = (
                v_new[j, rows - 1 :, at] - (courant * 0.5) * totals[1][j][s : s + 1]
            )
        copies.append(pltpu.make_async_copy(v_new.at[j], out_ref.at[j, 2], sems.at[j]))
        copies[-1].start()
    for copy in copies:
        copy.wait()


def body(
    sample_collection,
    seabed_profile,
    gauge_grid_position,
    observed_values,
    error_scale,
    perturbation,
    inflation,
):
    members, _, rows, columns = sample_collection.shape
    bands, mems = lax.axis_size("band"), lax.axis_size("mem")
    total_rows, total = rows * bands, members * mems
    padded = pad8(members)
    first_row = lax.axis_index("band") * rows
    row_index = first_row.reshape(1)

    field = jax.ShapeDtypeStruct((members, rows, columns), f32)
    edge = jax.ShapeDtypeStruct((members, 1, columns), f32)
    smem = pl.BlockSpec(memory_space=pltpu.SMEM)
    vmem = pl.BlockSpec(memory_space=pltpu.VMEM)
    hbm = pl.BlockSpec(memory_space=pl.ANY)
    size = 4 * members * rows * columns

    def call(kernel, ins, outs, shapes, limit, flops, moved, scratch=(), aliases={}):
        return pl.pallas_call(
            kernel,
            in_specs=ins,
            out_specs=outs,
            out_shape=shapes,
            scratch_shapes=list(scratch),
            input_output_aliases=aliases,
            compiler_params=pltpu.CompilerParams(vmem_limit_bytes=limit << 20),
            cost_estimate=cost(flops, moved),
        )

    x = sample_collection
    early = -(-2 * members // 3)
    halves = [count for count in (early, members - early) if count]
    fields = [jax.ShapeDtypeStruct((count, rows, columns), f32) for count in halves]
    even, odd = call(
        edge_kernel, [smem, hbm, hbm], [vmem] * 2, [edge, edge], 60, size, size,
        scratch=[
            pltpu.VMEM((members, rows, columns), f32),
            pltpu.VMEM((rows, columns), f32),
            pltpu.SemaphoreType.DMA((2,)),
        ],
    )(row_index, x, seabed_profile)
    even, odd = swap_edges(even, odd)
    code = call(
        functools.partial(index_kernel, rows, columns), [smem, vmem], vmem,
        jax.ShapeDtypeStruct(gauge_grid_position.shape, jnp.int32), 1, 10000, 4096,
    )(row_index, gauge_grid_position)
    h, u = call(
        functools.partial(begin_kernel, total_rows),
        [smem] + [vmem] * 2, [vmem] * 2, [field, field], 12, 20 * size, 4 * size,
    )(row_index, x, seabed_profile)
    h, u, even, odd = call(
        height_kernel,
        [smem] + [vmem] * 4, [vmem] * 4, [field, field, edge, edge], 12, 5 * size, 4 * size,
    )(row_index, h, u, even, odd)
    u_far = far_gather(u)
    even, odd = swap_edges(even, odd)
    even, odd, *v = call(
        functools.partial(speed_kernel, total_rows),
        [smem] + [vmem] * 6, [vmem] * (2 + len(halves)), [edge, edge, *fields], 12,
        30 * size, 6 * size,
    )(row_index, h, u, x, seabed_profile, even, odd)
    v_far = []
    for block in v:
        v_far.append(far_gather(block))
    even, odd = swap_edges(even, odd)

    lines = gauge_grid_position.shape[0]
    h = call(
        third_kernel, [vmem] * (3 + len(v)), vmem, field, 12, 10 * size, 4 * size,
    )(h, u, seabed_profile, *v)
    h, even, odd, predicted = call(
        probe_kernel,
        [smem, smem] + [vmem] * 3, [vmem] * 4,
        [field, edge, edge, jax.ShapeDtypeStruct((lines, padded, LANES), f32)], 12,
        20 * size, 4 * size,
        scratch=[pltpu.VMEM((members * rows * columns // LANES, LANES), f32)],
    )(row_index, code, h, even, odd)
    gathered = [predicted] + far_gather(predicted)
    if mems % 2 == 0:
        gathered = gathered + [near_swap(b) for b in gathered]
    n = len(gathered)
    height_rows = n * padded
    reach = -(-(height_rows + padded) // LANES) * LANES
    partial = call(
        functools.partial(gram_kernel, total, members),
        [smem] + [vmem] * (3 + n), vmem, jax.ShapeDtypeStruct((height_rows, reach), f32), 8,
        1000000, 200000,
        scratch=[
            pltpu.VMEM((height_rows, lines * LANES), f32),
            pltpu.VMEM((reach, lines * LANES), f32),
        ],
    )(inflation, observed_values, error_scale, perturbation, *gathered)
    summed = band_sum(partial)
    transform = call(
        functools.partial(solve_kernel, total, members, n),
        [smem, vmem], vmem, jax.ShapeDtypeStruct((height_rows, reach), f32), 4,
        1000000, 40000,
    )(inflation, summed)

    h_far = far_gather(h)
    even, odd = swap_edges(even, odd)
    rim = call(
        functools.partial(pack_kernel, rows), [smem] + [vmem] * 2, vmem,
        jax.ShapeDtypeStruct((members, 2, 8, columns // 8), f32), 4, size // 4, size // 2,
    )(row_index, even, odd)
    rim_far = far_gather(rim)

    def grouped(own, far):
        if mems % 2:
            return [own] + far
        own_near = near_swap(own)
        return [own] + far + [own_near] + [near_swap(b) for b in far]

    speeds, heights, rims = grouped(u, u_far), grouped(h, h_far), grouped(rim, rim_far)
    sides = [grouped(b, f) for b, f in zip(v, v_far)]
    every = [g * padded for g in range(n)]
    near = [0] if mems % 2 else [0, n // 2]
    far = [g for g in range(n) if g not in near]
    side_places, begin = [], 0
    for count in halves:
        side_places += [g + begin for g in every]
        begin += count
    width = math.gcd(512, columns)
    whole = jax.ShapeDtypeStruct((members, 3, rows, columns), f32)

    def blend(lists, blocks):
        return call(
            functools.partial(blend_kernel, lists, height_rows, width),
            [smem] + [vmem] * len(blocks), [vmem] * len(lists), [field] * len(lists),
            4 + 2 * n, 100 * size, 10 * size,
        )(transform, *blocks)

    u_sum, h_part = blend((every, [every[g] for g in near]), [*speeds, *(heights[g] for g in near)])
    (v_sum,) = blend((side_places,), [b for side in sides for b in side])
    h_new = call(
        functools.partial(settle_kernel, [every[g] for g in far], height_rows, width),
        [smem] + [vmem] * (1 + len(far)), vmem, field, 6 + n, 50 * size, 4 * size,
    )(transform, h_part, *(heights[g] for g in far))
    u_new, v_part = call(
        functools.partial(turn_kernel, total_rows),
        [smem] + [vmem] * 3, [vmem, vmem], [field, field], 8, 20 * size, 6 * size,
    )(row_index, h_new, u_sum, v_sum)
    return call(
        functools.partial(finish_kernel, every, height_rows),
        [smem] + [vmem] * (3 + n), hbm, whole, 4 + n,
        20 * size, 3 * size,
        scratch=[
            pltpu.VMEM((members, rows, columns), f32),
            pltpu.SemaphoreType.DMA((members + 2,)),
        ],
    )(transform, v_part, h_new, u_new, *rims)


def solution(mesh):
    in_specs = (
        P("mem", None, "band", None),
        P("band", None),
        P("band", None),
        P("band", None),
        P("band", None),
        P("mem", "band", None),
        P(),
    )
    out_specs = P("mem", None, "band", None)

    return jax.shard_map(body, mesh=mesh, in_specs=in_specs, out_specs=out_specs, check_vma=False)
```

```python
import functools
import math

import jax
import jax.numpy as jnp
from jax import lax
from jax.experimental import pallas as pl
from jax.experimental.pallas import tpu as pltpu
from jax.sharding import PartitionSpec as P


LANES = 128

courant = 0.5
coriolis_base = 0.15
coriolis_slope = 0.3


f32 = jnp.float32


def pad8(count):
    return -(-count // 8) * 8


def cost(flops, moved):
    return pl.CostEstimate(flops=flops, bytes_accessed=moved, transcendentals=0)


def swap_edges(even, odd):
    count = lax.axis_size("band")

    def pairs(start):
        first = [(i, i + 1) for i in range(start, count - 1, 2)]
        return first + [(j, i) for i, j in first]

    even = lax.ppermute(even, "band", pairs(0))
    odd = lax.ppermute(odd, "band", pairs(1))
    return even, odd


def pick(row_ref, rows, top, bottom):
    odd = lax.rem(lax.div(row_ref[0], rows), 2) == 1
    return jnp.where(odd, top, bottom), jnp.where(odd, bottom, top)


def band_sum(part):
    count = lax.axis_size("band")
    if count & (count - 1):
        return lax.psum(part, "band")
    step = 1
    while step < count:
        other = lax.ppermute(part, "band", [(i, i ^ step) for i in range(count)])
        part = part + other
        step *= 2
    return part


def mem_plan(count):
    if count % 2 or count == 1:
        return [(s, None) for s in range(1, count)]
    far = [(2 * s, None) for s in range(1, count // 2)]
    return far


def far_gather(block):
    count = lax.axis_size("mem")
    return [
        lax.ppermute(block, "mem", [(i, (i + s) % count) for i in range(count)])
        for s, _ in mem_plan(count)
    ]


def near_swap(block):
    count = lax.axis_size("mem")
    return lax.ppermute(block, "mem", [(i, i ^ 1) for i in range(count)])


def east(q):
    columns = q.shape[-1]
    return (pltpu.roll(q, columns - 1, 1) - pltpu.roll(q, 1, 1)) * 0.5


def north(q, above, below):
    rows = q.shape[0]
    index = lax.broadcasted_iota(jnp.int32, q.shape, 0)
    up = jnp.where(index == rows - 1, below, pltpu.roll(q, rows - 1, 0))
    down = jnp.where(index == 0, above, pltpu.roll(q, 1, 0))
    return (up - down) * 0.5


def spin(first_row, shape, total_rows):
    rows = (first_row + lax.broadcasted_iota(jnp.int32, shape, 0)).astype(f32)
    return coriolis_base + coriolis_slope * (rows + 0.5) / total_rows


def edge_kernel(row_ref, x_ref, b_ref, even_out, odd_out, speed, depth, sems):
    rows = b_ref.shape[0]
    copies = []
    for k, row in enumerate((0, rows - 1)):
        copies += [
            pltpu.make_async_copy(b_ref.at[pl.ds(row, 1)], depth.at[k], sems.at[2 * k]),
            pltpu.make_async_copy(x_ref.at[:, 2, pl.ds(row, 1)], speed.at[k], sems.at[2 * k + 1]),
        ]
    for copy in copies:
        copy.start()
    for copy in copies:
        copy.wait()

    def member(m, _):
        even_out[m], odd_out[m] = pick(
            row_ref, rows, depth[0] * speed[0, m], depth[1] * speed[1, m]
        )
        return 0

    lax.fori_loop(0, x_ref.shape[0], member, 0)


def index_kernel(rows, columns, row_ref, cell_ref, code_ref):
    row, column = split(cell_ref[...] - row_ref[0] * columns, columns)
    block, place = split(column, LANES)
    lane = lax.broadcasted_iota(jnp.int32, cell_ref.shape, 1)
    code_ref[...] = (block * rows + row) * LANES + ((lane - place) & (LANES - 1))


def begin_kernel(total_rows, row_ref, x_ref, b_ref, h_out, u_out):
    depth = b_ref[...]
    turn = spin(row_ref[0], depth.shape, total_rows)

    def member(m, _):
        u, v = x_ref[m, 1], x_ref[m, 2]
        h = x_ref[m, 0] - courant * (east(depth * u) + north(depth * v, 0.0, 0.0))
        h_out[m] = h
        u_out[m] = u - courant * east(h) + turn * v
        return 0

    lax.fori_loop(0, h_out.shape[0], member, 0)


def rim_rows(row_ref, shape, even, odd):
    rows = shape[0]
    above, below = pick(row_ref, rows, even, odd)
    index = lax.broadcasted_iota(jnp.int32, shape, 0)
    rim = jnp.where(index == 0, above, jnp.where(index == rows - 1, -below, 0.0))
    return (courant * 0.5) * rim


def height_kernel(
    row_ref, h_ref, u_ref, even_ref, odd_ref, h_out, u_out, even_out, odd_out
):
    rows = h_ref.shape[1]

    def member(m, _):
        rim = rim_rows(row_ref, h_ref.shape[1:], even_ref[m], odd_ref[m])
        h = h_ref[m] + rim
        h_out[m] = h
        even_out[m], odd_out[m] = pick(row_ref, rows, h[:1], h[-1:])
        u_out[m] = u_ref[m] - courant * east(rim)
        return 0

    lax.fori_loop(0, h_out.shape[0], member, 0)


def speed_kernel(
    total_rows, row_ref, h_ref, u_ref, x_ref, b_ref, even_ref, odd_ref, even_out, odd_out, *v_outs
):
    depth = b_ref[...]
    rows = depth.shape[0]
    turn = spin(row_ref[0], depth.shape, total_rows)
    base = 0
    for v_out in v_outs:

        def member(i, _, v_out=v_out, base=base):
            m = base + i
            above, below = pick(row_ref, rows, even_ref[m], odd_ref[m])
            v = x_ref[m, 2] - courant * north(h_ref[m], above, below) - turn * u_ref[m]
            v_out[i] = v
            flux = depth * v
            even_out[m], odd_out[m] = pick(row_ref, rows, flux[:1], flux[-1:])
            return 0

        lax.fori_loop(0, v_out.shape[0], member, 0)
        base += v_out.shape[0]


def split(value, by):
    if by & (by - 1):
        return lax.div(value, by), lax.rem(value, by)
    return lax.shift_right_logical(value, by.bit_length() - 1), value & (by - 1)


def third_kernel(h_ref, u_ref, b_ref, *refs):
    v_refs, h_out = refs[:-1], refs[-1]
    depth = b_ref[...]
    offset = 0
    for v_ref in v_refs:

        def member(i, _, v_ref=v_ref, offset=offset):
            m = offset + i
            h_out[m] = h_ref[m] - courant * (
                east(depth * u_ref[m]) + north(depth * v_ref[i], 0.0, 0.0)
            )
            return 0

        lax.fori_loop(0, v_ref.shape[0], member, 0)
        offset += v_ref.shape[0]


def probe_kernel(
    row_ref, code_ref, part_ref, even_ref, odd_ref, h_out, even_out, odd_out, out_ref, cells
):
    members, rows, columns = part_ref.shape
    stride = rows * columns // LANES

    def member(m, _):
        h = part_ref[m] + rim_rows(row_ref, (rows, columns), even_ref[m], odd_ref[m])
        h_out[m] = h
        even_out[m], odd_out[m] = pick(row_ref, rows, h[:1], h[-1:])
        base = pl.multiple_of(m * stride, 8)
        for c in range(columns // LANES):
            cells[pl.ds(base + c * rows, rows), :] = h[:, c * LANES : (c + 1) * LANES]
        return 0

    lax.fori_loop(0, members, member, 0)
    out_ref[...] = jnp.zeros_like(out_ref)
    lane = lax.broadcasted_iota(jnp.int32, (members, LANES), 1)
    for k in range(out_ref.shape[0]):

        def take(i, held, k=k):
            start, turn = split(code_ref[k, i], LANES)
            piece = cells[pl.ds(start, members, stride=stride), :]
            turned = pltpu.roll(piece, turn, 1)
            return jnp.where(lane == i, turned, held)

        out_ref[k, :members, :] = lax.fori_loop(
            0, LANES, take, jnp.zeros((members, LANES), f32), unroll=16
        )


def pack_kernel(rows, row_ref, *refs):
    ins, out_ref = refs[:-1], refs[-1]
    width = out_ref.shape[-1]

    def member(m, _):
        for k in range(0, len(ins), 2):
            for side, line in enumerate(pick(row_ref, rows, ins[k][m], ins[k + 1][m])):
                for s in range(8):
                    out_ref[m, k + side, s : s + 1, :] = line[:, s * width : (s + 1) * width]
        return 0

    lax.fori_loop(0, out_ref.shape[0], member, 0)


def gram_kernel(total, members, inf_ref, obs_ref, scale_ref, pert_ref, *refs):
    out_ref, spread, both = refs[-3:]
    groups = refs[:-3]
    padded = groups[0].shape[1]
    real = lax.broadcasted_iota(jnp.int32, (padded, LANES), 0) < members
    root = jnp.sqrt(jnp.full((1, LANES), inf_ref[0], f32))
    both[...] = jnp.zeros_like(both)
    for k in range(groups[0].shape[0]):
        at = slice(k * LANES, (k + 1) * LANES)
        scale = scale_ref[k : k + 1, :]
        sums = groups[0][k]
        for g in groups[1:]:
            sums = sums + g[k]
        centre = jnp.sum(sums, axis=0, keepdims=True) / total
        for n, g in enumerate(groups):
            s = jnp.where(real, (g[k] - centre) / (scale * math.sqrt(total - 1)), 0.0)
            spread[n * padded : (n + 1) * padded, at] = s
            both[n * padded : (n + 1) * padded, at] = s
        for m in range(members):
            both[len(groups) * padded + m : len(groups) * padded + m + 1, at] = (
                obs_ref[k : k + 1, :]
                + root * scale * pert_ref[m, k : k + 1, :]
                - groups[0][k, m : m + 1, :]
            ) / scale
    out_ref[...] = lax.dot_general(
        spread[...], both[...], (((1,), (1,)), ((), ())),
        precision=lax.Precision.HIGHEST, preferred_element_type=f32,
    )


def solve_kernel(total, members, groups, inf_ref, part_ref, out_ref):
    a = part_ref[...]
    size = a.shape[0]
    padded = size // groups
    row = lax.broadcasted_iota(jnp.int32, a.shape, 0)
    lane = lax.broadcasted_iota(jnp.int32, a.shape, 1)
    a = a + jnp.where(row == lane, inf_ref[0], 0.0)
    for g in range(groups):
        for m in range(members):
            k = g * padded + m
            pivot = a[k : k + 1, k : k + 1]
            inverse = 1.0 / jnp.sqrt(pivot)
            line = a[k : k + 1, :] * inverse
            column = a[:, k : k + 1] * inverse
            a = jnp.where(row == k, line, a - column * line)
    diagonal = jnp.sum(jnp.where(row == lane, a, 0.0), axis=1, keepdims=True)
    real = lax.rem(row, padded) < members
    w = jnp.where(real, a / diagonal, 0.0)
    mean = jnp.sum(w, axis=0, keepdims=True) / total
    unit = jnp.where(lane - size == row, 1.0, 0.0)
    out_ref[...] = unit + (w - mean) / math.sqrt(total - 1)


def weighted(t_ref, pieces, at, first, members, rows, width, start=None):
    total = list(start) if start is not None else [jnp.zeros((rows, width), f32)] * members
    for g, ref in pieces:
        for i in range(ref.shape[0]):
            value = ref[i, :, at]
            for j in range(members):
                total[j] = total[j] + t_ref[g + i, first + j] * value
    return total


def blend_kernel(lists, first, width, t_ref, *refs):
    outs = refs[-len(lists) :]
    members, rows, columns = outs[0].shape

    def chunk(c, _):
        at = pl.ds(pl.multiple_of(c * width, LANES), width)
        start = 0
        for places, out in zip(lists, outs):
            pieces = list(zip(places, refs[start:]))
            start += len(places)
            for j, t in enumerate(weighted(t_ref, pieces, at, first, members, rows, width)):
                out[j, :, at] = t
        return 0

    lax.fori_loop(0, columns // width, chunk, 0)


def settle_kernel(places, first, width, t_ref, part_ref, *refs):
    pieces = list(zip(places, refs))
    h_out = refs[len(places)]
    members, rows, columns = part_ref.shape

    def chunk(c, _):
        at = pl.ds(pl.multiple_of(c * width, LANES), width)
        start = [part_ref[j, :, at] for j in range(members)]
        for j, t in enumerate(weighted(t_ref, pieces, at, first, members, rows, width, start)):
            h_out[j, :, at] = t
        return 0

    lax.fori_loop(0, columns // width, chunk, 0)


def turn_kernel(total_rows, row_ref, h_ref, u_ref, v_ref, u_out, v_out):
    members, rows, columns = h_ref.shape
    turn = spin(row_ref[0], (rows, columns), total_rows)

    def member(j, _):
        h, v = h_ref[j], v_ref[j]
        u = u_ref[j] - courant * east(h) + turn * v
        u_out[j] = u
        v_out[j] = v - courant * north(h, 0.0, 0.0) - turn * u
        return 0

    lax.fori_loop(0, members, member, 0)


def packed_east(q):
    count, width = q.shape
    lane = lax.broadcasted_iota(jnp.int32, q.shape, 1)
    up, down = pltpu.roll(q, width - 1, 1), pltpu.roll(q, 1, 1)
    up = jnp.where(lane == width - 1, pltpu.roll(up, count - 1, 0), up)
    down = jnp.where(lane == 0, pltpu.roll(down, 1, 0), down)
    return (up - down) * 0.5


def rim_totals(t_ref, pieces, first, members, side, start):
    total = list(start)
    for g, ref in pieces:
        for i in range(members):
            value = ref[i, side]
            for j in range(members):
                total[j] = total[j] + t_ref[g + i, first + j] * value
    return total


def rim_kernel(places, first, t_ref, *refs):
    pieces, out_ref = list(zip(places, refs)), refs[-1]
    members, sides, _, width = out_ref.shape
    for side in range(sides):
        zeros = [jnp.zeros((8, width), f32)] * members
        for j, t in enumerate(rim_totals(t_ref, pieces, first, members, side, zeros)):
            out_ref[j, side] = t


def finish_kernel(places, first, total_rows, row_ref, t_ref, v_ref, h_ref, u_ref, part_ref, *refs):
    ins, (out_ref, v_new, u_new, sems) = refs[:-4], refs[-4:]
    members, rows, columns = v_ref.shape
    width = columns // 8
    copies = [pltpu.make_async_copy(h_ref, out_ref.at[:, 0], sems.at[2 * members])]
    copies[0].start()
    turn = spin(row_ref[0], (rows, width), total_rows)
    pieces = list(zip(places, ins))
    totals = [
        rim_totals(
            t_ref, pieces, first, members, side, [part_ref[j, side] for j in range(members)]
        )
        for side in range(4)
    ]
    for j in range(members):
        v_new[j] = v_ref[j]
        u_new[j] = u_ref[j]
        for side, sign, row in ((0, 1.0, 0), (1, -1.0, rows - 1)):
            at_row = slice(row, row + 1)
            u_term = (-sign * courant * courant * 0.5) * packed_east(totals[2 + side][j])
            v_term = (sign * courant * 0.5) * totals[side][j] - turn[at_row] * u_term
            for s in range(8):
                at = slice(s * width, (s + 1) * width)
                u_new[j, at_row, at] = u_new[j, at_row, at] + u_term[s : s + 1]
                v_new[j, at_row, at] = v_new[j, at_row, at] + v_term[s : s + 1]
        for q, ref in ((1, u_new), (2, v_new)):
            copies.append(
                pltpu.make_async_copy(
                    ref.at[j], out_ref.at[j, q], sems.at[(q - 1) * members + j]
                )
            )
            copies[-1].start()
    for copy in copies:
        copy.wait()


def body(
    sample_collection,
    seabed_profile,
    gauge_grid_position,
    observed_values,
    error_scale,
    perturbation,
    inflation,
):
    members, _, rows, columns = sample_collection.shape
    bands, mems = lax.axis_size("band"), lax.axis_size("mem")
    total_rows, total = rows * bands, members * mems
    padded = pad8(members)
    first_row = lax.axis_index("band") * rows
    row_index = first_row.reshape(1)

    field = jax.ShapeDtypeStruct((members, rows, columns), f32)
    edge = jax.ShapeDtypeStruct((members, 1, columns), f32)
    smem = pl.BlockSpec(memory_space=pltpu.SMEM)
    vmem = pl.BlockSpec(memory_space=pltpu.VMEM)
    hbm = pl.BlockSpec(memory_space=pl.ANY)
    size = 4 * members * rows * columns

    def call(kernel, ins, outs, shapes, limit, flops, moved, scratch=(), aliases={}):
        return pl.pallas_call(
            kernel,
            in_specs=ins,
            out_specs=outs,
            out_shape=shapes,
            scratch_shapes=list(scratch),
            input_output_aliases=aliases,
            compiler_params=pltpu.CompilerParams(vmem_limit_bytes=limit << 20),
            cost_estimate=cost(flops, moved),
        )

    x = sample_collection
    early = -(-2 * members // 3)
    halves = [count for count in (early, members - early) if count]
    fields = [jax.ShapeDtypeStruct((count, rows, columns), f32) for count in halves]
    even, odd = call(
        edge_kernel, [smem, hbm, hbm], [vmem] * 2, [edge, edge], 60, size, size,
        scratch=[
            pltpu.VMEM((2, members, 1, columns), f32),
            pltpu.VMEM((2, 1, columns), f32),
            pltpu.SemaphoreType.DMA((4,)),
        ],
    )(row_index, x, seabed_profile)
    even, odd = swap_edges(even, odd)
    first_rim = [even, odd]
    code = call(
        functools.partial(index_kernel, rows, columns), [smem, vmem], vmem,
        jax.ShapeDtypeStruct(gauge_grid_position.shape, jnp.int32), 1, 10000, 4096,
    )(row_index, gauge_grid_position)
    h, u_part = call(
        functools.partial(begin_kernel, total_rows),
        [smem] + [vmem] * 2, [vmem] * 2, [field, field], 12, 20 * size, 4 * size,
    )(row_index, x, seabed_profile)
    u_far = far_gather(u_part)
    h, u, even, odd = call(
        height_kernel,
        [smem] + [vmem] * 4, [vmem] * 4, [field, field, edge, edge], 12, 5 * size, 4 * size,
    )(row_index, h, u_part, even, odd)
    even, odd = swap_edges(even, odd)
    even, odd, *v = call(
        functools.partial(speed_kernel, total_rows),
        [smem] + [vmem] * 6, [vmem] * (2 + len(halves)), [edge, edge, *fields], 12,
        30 * size, 6 * size,
    )(row_index, h, u, x, seabed_profile, even, odd)
    v_far = []
    for block in v:
        v_far.append(far_gather(block))
    even, odd = swap_edges(even, odd)

    lines = gauge_grid_position.shape[0]
    h = call(
        third_kernel, [vmem] * (3 + len(v)), vmem, field, 12, 10 * size, 4 * size,
    )(h, u, seabed_profile, *v)
    h, even, odd, predicted = call(
        probe_kernel,
        [smem, smem] + [vmem] * 3, [vmem] * 4,
        [field, edge, edge, jax.ShapeDtypeStruct((lines, padded, LANES), f32)], 12,
        20 * size, 4 * size,
        scratch=[pltpu.VMEM((members * rows * columns // LANES, LANES), f32)],
    )(row_index, code, h, even, odd)
    gathered = [predicted] + far_gather(predicted)
    if mems % 2 == 0:
        gathered = gathered + [near_swap(b) for b in gathered]
    n = len(gathered)
    height_rows = n * padded
    reach = -(-(height_rows + padded) // LANES) * LANES
    partial = call(
        functools.partial(gram_kernel, total, members),
        [smem] + [vmem] * (3 + n), vmem, jax.ShapeDtypeStruct((height_rows, reach), f32), 8,
        1000000, 200000,
        scratch=[
            pltpu.VMEM((height_rows, lines * LANES), f32),
            pltpu.VMEM((reach, lines * LANES), f32),
        ],
    )(inflation, observed_values, error_scale, perturbation, *gathered)
    summed = band_sum(partial)
    transform = call(
        functools.partial(solve_kernel, total, members, n),
        [smem, vmem], vmem, jax.ShapeDtypeStruct((height_rows, reach), f32), 4,
        1000000, 40000,
    )(inflation, summed)

    h_far = far_gather(h)
    even, odd = swap_edges(even, odd)
    rim = call(
        functools.partial(pack_kernel, rows), [smem] + [vmem] * 4, vmem,
        jax.ShapeDtypeStruct((members, 4, 8, columns // 8), f32), 4, size // 4, size // 2,
    )(row_index, even, odd, *first_rim)
    rim_far = far_gather(rim)

    def grouped(own, far):
        if mems % 2:
            return [own] + far
        own_near = near_swap(own)
        return [own] + far + [own_near] + [near_swap(b) for b in far]

    speeds, heights, rims = grouped(u_part, u_far), grouped(h, h_far), grouped(rim, rim_far)
    sides = [grouped(b, f) for b, f in zip(v, v_far)]
    every = [g * padded for g in range(n)]
    near = [0] if mems % 2 else [0, n // 2]
    far = [g for g in range(n) if g not in near]
    side_places, begin = [], 0
    for count in halves:
        side_places += [g + begin for g in every]
        begin += count
    width = math.gcd(512, columns)
    whole = jax.ShapeDtypeStruct((members, 3, rows, columns), f32)

    def blend(lists, blocks):
        return call(
            functools.partial(blend_kernel, lists, height_rows, width),
            [smem] + [vmem] * len(blocks), [vmem] * len(lists), [field] * len(lists),
            4 + 2 * n, 100 * size, 10 * size,
        )(transform, *blocks)

    u_sum, h_part = blend((every, [every[g] for g in near]), [*speeds, *(heights[g] for g in near)])
    (v_sum,) = blend((side_places,), [b for side in sides for b in side])
    h_new = call(
        functools.partial(settle_kernel, [every[g] for g in far], height_rows, width),
        [smem] + [vmem] * (1 + len(far)), vmem, field, 6 + n, 50 * size, 4 * size,
    )(transform, h_part, *(heights[g] for g in far))
    u_new, v_part = call(
        functools.partial(turn_kernel, total_rows),
        [smem] + [vmem] * 3, [vmem, vmem], [field, field], 8, 20 * size, 6 * size,
    )(row_index, h_new, u_sum, v_sum)
    rim_part = call(
        functools.partial(rim_kernel, [every[g] for g in near], height_rows),
        [smem] + [vmem] * len(near), vmem, jax.ShapeDtypeStruct(rim.shape, f32), 4,
        10 * size, size,
    )(transform, *(rims[g] for g in near))
    return call(
        functools.partial(finish_kernel, [every[g] for g in far], height_rows, total_rows),
        [smem] * 2 + [vmem] * (4 + len(far)), hbm, whole, 6 + n,
        20 * size, 3 * size,
        scratch=[
            pltpu.VMEM((members, rows, columns), f32),
            pltpu.VMEM((members, rows, columns), f32),
            pltpu.SemaphoreType.DMA((2 * members + 1,)),
        ],
    )(row_index, transform, v_part, h_new, u_new, rim_part, *(rims[g] for g in far))


def solution(mesh):
    in_specs = (
        P("mem", None, "band", None),
        P("band", None),
        P("band", None),
        P("band", None),
        P("band", None),
        P("mem", "band", None),
        P(),
    )
    out_specs = P("mem", None, "band", None)

    return jax.shard_map(body, mesh=mesh, in_specs=in_specs, out_specs=out_specs, check_vma=False)
```
